32 devices in a mesh: section: 2 (over core), seq: 4 (over y, x), tensor: 4 (over z).
Axes of the slice: x: 2, y: 2, z: 4, core: 2. Of those that a mesh axis runs over, the one named last changes fastest.
Arguments:
- tokens: bfloat16 [4096, 1024], P('seq', 'tensor'), may hold values from -6 to 6
- segments: int32 [8, 512], P('seq'), may hold values from 0 to 3, never falling along the last dimension, each value on 1 to 256 neighbouring positions
- cotangent: bfloat16 [4096, 1024], P('seq', 'tensor'), may hold values from -6 to 6
- norm1_gain: bfloat16 [2, 1024], P('section', ('tensor', 'seq')), may hold values from 0.5 to 1.5
- norm1_bias: bfloat16 [2, 1024], P('section', ('tensor', 'seq')), may hold values from -3 to 3
- qkv_weight: bfloat16 [2, 1024, 16, 192], P('section', 'seq', 'tensor'), may hold values from -0.1875 to 0.1875
- qv_bias: bfloat16 [2, 16, 128], P('section', 'tensor', 'seq'), may hold values from -4 to 4
- out_weight: bfloat16 [2, 16, 64, 1024], P('section', 'tensor', None, 'seq'), may hold values from -0.75 to 0.75
- out_bias: bfloat16 [2, 1024], P('section', ('tensor', 'seq')), may hold values from -3 to 3
- norm2_gain: bfloat16 [2, 1024], P('section', ('tensor', 'seq')), may hold values from 0.5 to 1.5
- norm2_bias: bfloat16 [2, 1024], P('section', ('tensor', 'seq')), may hold values from -3 to 3
- up_weight: bfloat16 [2, 1024, 4096], P('section', 'seq', 'tensor'), may hold values from -0.1875 to 0.1875
- up_bias: bfloat16 [2, 4096], P('section', ('tensor', 'seq')), may hold values from -4 to 4
- down_weight: bfloat16 [2, 4096, 1024], P('section', 'tensor', 'seq'), may hold values from -0.09375 to 0.09375
- down_bias: bfloat16 [2, 1024], P('section', ('tensor', 'seq')), may hold values from -3 to 3
Outputs:
- section_out: bfloat16 [2, 4096, 1024], P('section', 'seq', 'tensor')
- input_grad: bfloat16 [2, 4096, 1024], P('section', 'seq', 'tensor')
- grad_norm1_gain: float32 [2, 1024], P('section', ('tensor', 'seq'))
- grad_norm1_bias: float32 [2, 1024], P('section', ('tensor', 'seq'))
- grad_qkv_weight: float32 [2, 1024, 16, 192], P('section', 'seq', 'tensor')
- grad_qv_bias: float32 [2, 16, 128], P('section', 'tensor', 'seq')
- grad_out_weight: float32 [2, 16, 64, 1024], P('section', 'tensor', None, 'seq')
- grad_out_bias: float32 [2, 1024], P('section', ('tensor', 'seq'))
- grad_norm2_gain: float32 [2, 1024], P('section', ('tensor', 'seq'))
- grad_norm2_bias: float32 [2, 1024], P('section', ('tensor', 'seq'))
- grad_up_weight: float32 [2, 1024, 4096], P('section', 'seq', 'tensor')
- grad_up_bias: float32 [2, 4096], P('section', ('tensor', 'seq'))
- grad_down_weight: float32 [2, 4096, 1024], P('section', 'tensor', 'seq')
- grad_down_bias: float32 [2, 1024], P('section', ('tensor', 'seq'))
The draws below stay inside these ranges and needn't reach their ends.
Inputs may be any that keep to these rules, and one draw needn't show every extreme that they name: `segments`: along each sequence the document numbers never fall; every document holds 1 to 256 positions.
All inputs are finite; a program needn't handle non-finite values.
Results may differ from the reference program's by a relative error of at most 0.02.
Values may be sent and summed in bfloat16 or wider, within the bound.
A program may use at most 192 MiB of HBM per device.

```python
import math
import jax
import jax.numpy as jnp
import numpy as np
from jax import lax

D = 1024
H = 16
HD = 64
FF = 4096
LEN = 512
DOCS = 4
LAYERS = 2
SEQS = 8
TOKENS = 4096


def level_of(own_key, extent, split, smallest, high):
    def one(axis_at, shards_of):
        heights = jax.random.uniform(jax.random.fold_in(jax.random.fold_in(own_key, 6), axis_at), (shards_of,), jnp.float32, smallest / len(split), high / len(split))
        return jnp.repeat(jnp.exp(heights), extent[axis_at] // shards_of).reshape((-1,) + (1,) * (len(extent) - axis_at - 1))

    loudness = one(*split[0])
    for cut in split[1:]:
        loudness = loudness * one(*cut)
    return loudness


def split_up(count, total, most, skew):
    weights = [(1 << 20) // math.isqrt(standing ** skew) + 1 for standing in range(2, count + 1)]
    spare, counts = total - most - (count - 1), [1] * (count - 1)
    while spare > 0:
        free = [i for i in range(count - 1) if counts[i] < most]
        mass, remaining = sum([weights[i] for i in free]), spare
        for i in free:
            addition = min(most - counts[i], max(1, remaining * weights[i] // mass), spare)
            counts[i] = counts[i] + addition
            spare = spare - addition
    return np.array([most] + counts)


def ragged_sizes(rng, number_of, total, most, lean):
    if number_of == 2:
        one = jax.random.randint(rng, (), max(1, total - most), min(most, total - 1) + 1)
        return jnp.stack([one, total - one])
    sizes = jnp.asarray(split_up(number_of, total, most, lean), jnp.int32)
    twos = (number_of - 1) // 2
    donor, taker = sizes[1:1 + 2 * twos:2], sizes[2:2 + 2 * twos:2]
    margin = jnp.minimum(donor - 1, most - taker)
    passed = jax.random.randint(jax.random.fold_in(rng, 1), (twos,), 0, 1 << 20) % (margin + 1)
    sizes = sizes.at[1:1 + 2 * twos:2].set(donor - passed).at[2:2 + 2 * twos:2].set(taker + passed)
    return sizes[jax.random.permutation(jax.random.fold_in(rng, 2), number_of)]


def normal_values(key, shape, spread, most, cuts=(), kind=jnp.bfloat16):
    drawn = spread * jax.random.normal(key, shape, jnp.float32)
    if cuts:
        drawn = drawn * level_of(key, shape, cuts, -0.22, 0.18)
    return jnp.clip(drawn, -most, most).astype(kind)


def setup_inputs(seed: int = 0) -> dict:
    key_list = jax.random.split(jax.random.key(seed), 16)
    tokens = normal_values(key_list[0], (TOKENS, D), 1.0, 6.0, ((0, 4), (1, 4)))
    segments = jax.vmap(lambda own: jnp.searchsorted(jnp.cumsum(ragged_sizes(own, DOCS, LEN, LEN // 2, 1)), jnp.arange(LEN), side="right"))(jax.random.split(key_list[1], SEQS)).reshape((SEQS, LEN)).astype(jnp.int32)
    cotangent = normal_values(key_list[2], (TOKENS, D), 1.0, 6.0, ((0, 4), (1, 4)))
    norm1_gain = jnp.clip(1.0 + 0.1 * jax.random.normal(key_list[3], (LAYERS, D), jnp.float32), 0.5, 1.5).astype(jnp.bfloat16)
    norm1_bias = normal_values(key_list[4], (LAYERS, D), 0.3, 3.0, ((0, 2), (1, 16)))
    qkv_weight = normal_values(key_list[5], (LAYERS, D, H, 3 * HD), D ** -0.5, 0.1875, ((0, 2), (1, 4), (2, 4)))
    qv_bias = normal_values(key_list[6], (LAYERS, H, 2 * HD), 0.5, 4.0, ((0, 2), (1, 4), (2, 4)))
    out_weight = normal_values(key_list[7], (LAYERS, H, HD, D), (D // 16) ** -0.5, 0.75, ((0, 2), (1, 4), (3, 4)))
    out_bias = normal_values(key_list[8], (LAYERS, D), 0.3, 3.0, ((0, 2), (1, 16)))
    norm2_gain = jnp.clip(1.0 + 0.1 * jax.random.normal(key_list[9], (LAYERS, D), jnp.float32), 0.5, 1.5).astype(jnp.bfloat16)
    norm2_bias = normal_values(key_list[10], (LAYERS, D), 0.3, 3.0, ((0, 2), (1, 16)))
    up_weight = normal_values(key_list[11], (LAYERS, D, FF), D ** -0.5, 0.1875, ((0, 2), (1, 4), (2, 4)))
    up_bias = normal_values(key_list[12], (LAYERS, FF), 0.5, 4.0, ((0, 2), (1, 16)))
    down_weight = normal_values(key_list[13], (LAYERS, FF, D), FF ** -0.5, 0.09375, ((0, 2), (1, 4), (2, 4)))
    down_bias = normal_values(key_list[14], (LAYERS, D), 0.3, 3.0, ((0, 2), (1, 16)))
    return {"tokens": tokens, "segments": segments, "cotangent": cotangent, "norm1_gain": norm1_gain, "norm1_bias": norm1_bias, "qkv_weight": qkv_weight, "qv_bias": qv_bias, "out_weight": out_weight, "out_bias": out_bias, "norm2_gain": norm2_gain, "norm2_bias": norm2_bias, "up_weight": up_weight, "up_bias": up_bias, "down_weight": down_weight, "down_bias": down_bias}


@jax.custom_vjp
def low(v):
    return lax.optimization_barrier(v.astype(jnp.bfloat16)).astype(jnp.float32)

@jax.custom_vjp
def low_back(v):
    return v

def low_keep(v):
    return (low(v), None)

def low_pass(kept, grad):
    return (grad,)

def back_keep(v):
    return (v, None)

def back_low(kept, grad):
    return (low(grad),)
low.defvjp(low_keep, low_pass)
low_back.defvjp(back_keep, back_low)
epsilon = 1e-05
highest = lax.Precision.HIGHEST

def layer_norm(value, gain, shift):
    average = lax.optimization_barrier(jnp.mean(value, axis=-1, keepdims=True))
    variance = lax.optimization_barrier(jnp.mean(value * value, axis=-1, keepdims=True)) - average * average
    return (value - average) * lax.rsqrt(variance + epsilon) * gain + shift

def attend_one(query, keys, values, segment):
    factor = 1.0 / math.sqrt(HD)
    scores = low_back(jnp.einsum('qhe,khe->hqk', query, keys, precision=highest) * factor)
    place = jnp.arange(LEN)
    allowed = (place[None, :] <= place[:, None]) & (segment[:, None] == segment[None, :])
    masked = jnp.where(allowed[None], scores, -1e+30)
    highest_score = lax.optimization_barrier(jnp.max(masked, axis=-1, keepdims=True))
    raised = jnp.exp(masked - highest_score)
    chance = low(raised / lax.optimization_barrier(jnp.sum(raised, axis=-1, keepdims=True)))
    return jnp.einsum('hqk,khe->qhe', chance, values, precision=highest)

def layer(inputs, segs, params):
    gain1, bias1, w_qkv, b_qv, w_out, b_out, gain2, bias2, w_up, b_up, w_down, b_down = params
    rows = low_back(inputs)
    normed = low(layer_norm(rows, gain1, bias1))
    mixed = jnp.einsum('nd,dhe->nhe', normed, w_qkv, precision=highest)
    query = low(low_back(mixed[..., :HD] + b_qv[:, :HD]))
    keys = low(low_back(mixed[..., HD:2 * HD]))
    values = low(low_back(mixed[..., 2 * HD:] + b_qv[:, HD:]))
    count = rows.shape[0] // LEN
    shape4 = (count, LEN, H, HD)
    attend_saved = jax.checkpoint(attend_one)

    def one_sequence(item):
        return attend_saved(item[0], item[1], item[2], item[3])
    context = lax.map(one_sequence, (query.reshape(shape4), keys.reshape(shape4), values.reshape(shape4), segs))
    context = low(low_back(context.reshape(rows.shape[0], H * HD)))
    attn = low_back(jnp.dot(context, w_out.reshape(H * HD, D), precision=highest) + b_out)
    hidden = rows + attn
    normed2 = low(layer_norm(hidden, gain2, bias2))
    upper = low_back(jnp.dot(normed2, w_up, precision=highest) + b_up)
    active = low(jax.nn.gelu(upper, approximate=True))
    branch = low_back(jnp.dot(active, w_down, precision=highest) + b_down)
    return low(hidden + branch)

def reference(tokens, segments, cotangent, norm1_gain, norm1_bias, qkv_weight, qv_bias, out_weight, out_bias, norm2_gain, norm2_bias, up_weight, up_bias, down_weight, down_bias):
    params = (norm1_gain, norm1_bias, qkv_weight, qv_bias, out_weight, out_bias, norm2_gain, norm2_bias, up_weight, up_bias, down_weight, down_bias)
    params = tuple((item.astype(jnp.float32) for item in params))
    first = tuple((item[0] for item in params))
    second = tuple((item[1] for item in params))
    group = math.gcd(SEQS, 8)
    count = SEQS // group
    blocks = tokens.astype(jnp.float32).reshape(count, group * LEN, D)
    backs = cotangent.astype(jnp.float32).reshape(count, group * LEN, D)
    segs_all = segments.reshape(count, group, LEN)

    def step(carry, item):
        block, segs, back = item

        def section_fn(value, weights):
            return layer(value, segs, weights)
        middle, pull_first = jax.vjp(section_fn, block, first)
        final, pull_second = jax.vjp(section_fn, middle, second)
        grad_middle, grad_second = pull_second(back)
        grad_block, grad_first = pull_first(grad_middle)
        total_first = jax.tree.map(lambda acc, new: acc + new, carry[0], grad_first)
        total_second = jax.tree.map(lambda acc, new: acc + new, carry[1], grad_second)
        return ((total_first, total_second), (middle, final, grad_block, grad_middle))
    start = (jax.tree.map(jnp.zeros_like, first), jax.tree.map(jnp.zeros_like, second))
    totals, stacked = lax.scan(step, start, (blocks, segs_all, backs))
    middle, final, grad_block, grad_middle = (item.reshape(TOKENS, D) for item in stacked)
    section_out = jnp.stack([middle, final]).astype(jnp.bfloat16)
    input_grad = jnp.stack([grad_block, grad_middle]).astype(jnp.bfloat16)
    grads = tuple((jnp.stack([one, two]) for one, two in zip(totals[0], totals[1])))
    return (section_out, input_grad, grads[0], grads[1], grads[2], grads[3], grads[4], grads[5], grads[6], grads[7], grads[8], grads[9], grads[10], grads[11])
```

```python
import math

import jax
import jax.numpy as jnp
from jax import lax
from jax.experimental import pallas as pl
from jax.experimental.pallas import tpu as pltpu
from jax.sharding import PartitionSpec as P

epsilon = 1e-05
floor_value = -1e30
f32 = jnp.float32
bf16 = jnp.bfloat16
MESH = pl.DeviceIdType.MESH
CHUNKS = 4
STEP = 16


class Group:
    def __init__(self, number):
        self.number = number
        self.ins, self.in_specs = [], []
        self.outs, self.out_specs = [], []
        self.scratch = []
        self.count = 0
        self.jobs = []
        self.peers = set()

    def operand(self, value, space):
        self.ins.append(value)
        self.in_specs.append(pl.BlockSpec(memory_space=space))
        return ("in", len(self.ins) - 1)

    def result(self, shape, dtype, space):
        self.outs.append(jax.ShapeDtypeStruct(shape, dtype))
        self.out_specs.append(pl.BlockSpec(memory_space=space))
        return ("out", len(self.outs) - 1)

    def room(self, shape, dtype):
        self.scratch.append(pltpu.VMEM(shape, dtype))
        return ("tmp", len(self.scratch) - 1)

    def sems(self, count):
        first = self.count
        self.count += count
        return first

    def run(self):
        n_in, n_out, n_tmp = len(self.ins), len(self.outs), len(self.scratch)

        def kernel(*refs):
            banks = {
                "in": refs[:n_in],
                "out": refs[n_in : n_in + n_out],
                "tmp": refs[n_in + n_out : n_in + n_out + n_tmp],
            }
            env = Env(banks, refs[-2], refs[-1])
            env.greet(self.peers)
            stages = []
            for job in self.jobs:
                stages.extend(job(env))
            stages.sort(key=lambda item: item[0])
            for _, stage in stages:
                stage()
            env.finish()

        return pl.pallas_call(
            kernel,
            out_shape=tuple(self.outs),
            in_specs=self.in_specs,
            out_specs=tuple(self.out_specs),
            scratch_shapes=self.scratch
            + [pltpu.SemaphoreType.DMA((self.count,)), pltpu.SemaphoreType.DMA((self.count,))],
            compiler_params=pltpu.CompilerParams(
                collective_id=self.number, has_side_effects=True, vmem_limit_bytes=48 << 20
            ),
        )(*self.ins)


class Env:
    def __init__(self, banks, send, recv):
        self.banks, self.send, self.recv = banks, send, recv
        self.core = lax.axis_index("section")
        self.quad = lax.axis_index("seq")
        self.place = lax.axis_index("tensor")
        self.cores = lax.axis_size("section")
        self.quads = lax.axis_size("seq")
        self.places = lax.axis_size("tensor")
        self.pending = []

    def __call__(self, name):
        return self.banks[name[0]][name[1]]

    def greet(self, peers):
        barrier = pltpu.get_barrier_semaphore()
        total = 0
        if "plane" in peers:
            for core in range(2):
                for j in range(self.quads):
                    if core == 0 and j == 0:
                        continue
                    pl.semaphore_signal(
                        barrier, inc=1, device_id=self.peer(j, core), device_id_type=MESH
                    )
                    total += 1
        if "line" in peers:
            for j in range(1, self.places):
                pl.semaphore_signal(barrier, inc=1, device_id=self.along(j), device_id_type=MESH)
                total += 1
        elif "next" in peers:
            for shift in (-1, 1):
                there = self.place + shift

                @pl.when((there >= 0) & (there < self.places))
                def _():
                    pl.semaphore_signal(
                        barrier, inc=1, device_id={"tensor": there}, device_id_type=MESH
                    )

            edge = (self.place == 0) | (self.place == self.places - 1)
            amount = total

            @pl.when(edge)
            def _():
                pl.semaphore_wait(barrier, amount + 1)

            @pl.when(jnp.logical_not(edge))
            def _():
                pl.semaphore_wait(barrier, amount + 2)

            return
        pl.semaphore_wait(barrier, total)

    def peer(self, j, flip):
        target = {"seq": lax.rem(self.quad + j, self.quads)}
        target["section"] = (1 - self.core) if flip else self.core
        return target

    def along(self, j):
        return {"tensor": lax.rem(self.place + j, self.places)}

    def copy(self, source, target, sem, device):
        return pltpu.make_async_remote_copy(
            src_ref=source,
            dst_ref=target,
            send_sem=self.send.at[sem],
            recv_sem=self.recv.at[sem],
            device_id=device,
            device_id_type=MESH,
        )

    def start(self, source, target, sem, device, when=None):
        made = self.copy(source, target, sem, device)
        if when is None:
            made.start()
        else:
            pl.when(when)(made.start)
        self.pending.append((made.wait_send, when))

    def arrived(self, target, sem):
        self.copy(target, target, sem, {"section": 1 - self.core}).wait_recv()

    def local(self, source, target, sem, when=None):
        made = pltpu.make_async_copy(source, target, self.send.at[sem])
        if when is None:
            made.start()
        else:
            pl.when(when)(made.start)
        self.pending.append((made.wait, when))

    def finish(self):
        for wait, when in self.pending:
            if when is None:
                wait()
            else:
                pl.when(when)(wait)


def rows_loop(count, step, work):
    def one(i, carry):
        work(pl.multiple_of(i * step, step))
        return carry

    lax.fori_loop(0, count // step, one, 0)


def statistics(rows):
    average = jnp.mean(rows, axis=1, keepdims=True)
    variance = jnp.mean(rows * rows, axis=1, keepdims=True) - average * average
    scale = lax.rsqrt(variance + epsilon)
    return ((rows - average) * scale, scale)


def norm_backward(grad, centred, scale, gain):
    scaled = grad * gain
    total = jnp.mean(scaled, axis=1, keepdims=True)
    along = jnp.mean(scaled * centred, axis=1, keepdims=True)
    return scale * (scaled - total - centred * along)


def chain_sum(group, kind, partial, vectors, whole_in=None, half_in=None):
    count, width = partial.shape
    half = count // 2
    chunk = half // CHUNKS
    group.peers.add("next")
    n_part = group.operand(partial, pltpu.VMEM)
    n_vec = group.operand(vectors, pltpu.VMEM)
    n_wide = group.operand(whole_in, pltpu.VMEM) if whole_in is not None else None
    n_half = group.operand(half_in, pltpu.VMEM) if half_in is not None else None
    n_out = group.result((count, width), bf16, pltpu.VMEM)
    n_keep = group.result((half, width), f32, pltpu.VMEM) if kind in ("f1", "b1") else None
    sums = {"f1": 0, "f2": 0, "b1": 4, "b2": 2}[kind]
    n_sums = group.result((sums * 8, width), f32, pltpu.VMEM) if sums else None
    n_land = group.room((2, half, width), bf16)
    n_go = group.room((2, half, width), bf16)
    base = group.sems(4 * CHUNKS)

    def job(env):
        part, vec, out, land, go = env(n_part), env(n_vec), env(n_out), env(n_land), env(n_go)
        wide = env(n_wide) if n_wide else None
        kept = env(n_half) if n_half else None
        keep = env(n_keep) if n_keep else None
        acc = env(n_sums) if n_sums else None
        last = env.places - 1
        if acc is not None:
            acc[...] = jnp.zeros_like(acc)

        def add(row, value):
            acc[row * 8 : row * 8 + 8, :] += jnp.sum(
                value.reshape(STEP // 8, 8, width), axis=0
            )

        def close(side, k):
            first = side * half + k * chunk

            def work(i):
                at = pl.ds(pl.multiple_of(first + i, STEP), STEP)
                own = pl.ds(pl.multiple_of(k * chunk + i, STEP), STEP)
                total = land[side, own, :].astype(f32) + part[at, :].astype(f32)
                if kind == "f1":
                    hidden = wide[at, :].astype(f32) + (total + vec[0:1, :])
                    keep[own, :] = hidden
                    centred, _ = statistics(hidden)
                    out[at, :] = (centred * vec[1:2, :] + vec[2:3, :]).astype(bf16)
                elif kind == "f2":
                    out[at, :] = (kept[own, :] + (total + vec[0:1, :])).astype(bf16)
                elif kind == "b1":
                    centred, scale = statistics(kept[own, :])
                    upstream = wide[at, :].astype(f32)
                    grad = upstream + norm_backward(total, centred, scale, vec[0:1, :])
                    keep[own, :] = grad
                    low = grad.astype(bf16)
                    out[at, :] = low
                    add(0, total * centred)
                    add(1, total)
                    add(2, low.astype(f32))
                    add(3, upstream)
                else:
                    centred, scale = statistics(wide[at, :].astype(f32))
                    grad = kept[own, :] + norm_backward(total, centred, scale, vec[0:1, :])
                    out[at, :] = grad.astype(bf16)
                    add(0, total * centred)
                    add(1, total)

            rows_loop(chunk, STEP, work)

        stages = []
        for q in range(env.places):
            here = env.place == q
            for side, move in ((0, 1), (1, -1)):
                source, sink = (0, last) if side == 0 else (last, 0)
                steps_in = q if side == 0 else last - q
                steps_back = last + (last - steps_in)
                for k in range(CHUNKS):
                    at = pl.ds(side * half + k * chunk, chunk)
                    own = pl.ds(k * chunk, chunk)
                    sem = base + (side * 2) * CHUNKS + k
                    back = base + (side * 2 + 1) * CHUNKS + k

                    def forward(
                        q=q, here=here, side=side, move=move, source=source, sink=sink, k=k,
                        at=at, own=own, sem=sem, back=back,
                    ):
                        def act():
                            if q != source:
                                env.arrived(land.at[side, own, :], sem)
                            if q == sink:
                                close(side, k)
                                env.copy(
                                    out.at[at, :], out.at[at, :], back, {"tensor": q - move}
                                ).start()
                            else:
                                if q == source:
                                    sent = part.at[at, :]
                                else:

                                    def work(i):
                                        i_at = pl.ds(
                                            pl.multiple_of(side * half + k * chunk + i, STEP), STEP
                                        )
                                        i_own = pl.ds(pl.multiple_of(k * chunk + i, STEP), STEP)
                                        go[side, i_own, :] = (
                                            land[side, i_own, :].astype(f32)
                                            + part[i_at, :].astype(f32)
                                        ).astype(bf16)

                                    rows_loop(chunk, STEP, work)
                                    sent = go.at[side, own, :]
                                env.copy(
                                    sent, land.at[side, own, :], sem, {"tensor": q + move}
                                ).start()

                        pl.when(here)(act)

                    def backward(
                        q=q, here=here, move=move, source=source, at=at, back=back,
                    ):
                        def act():
                            env.arrived(out.at[at, :], back)
                            if q != source:
                                env.copy(
                                    out.at[at, :], out.at[at, :], back, {"tensor": q - move}
                                ).start()

                        pl.when(here)(act)

                    stages.append((k + steps_in, forward))
                    if q != sink:
                        stages.append((k + steps_back, backward))

        def drain():
            for q in range(env.places):

                def act(q=q):
                    for side, move in ((0, 1), (1, -1)):
                        source, sink = (0, last) if side == 0 else (last, 0)
                        for k in range(CHUNKS):
                            at = pl.ds(side * half + k * chunk, chunk)
                            sem = base + (side * 2) * CHUNKS + k
                            back = base + (side * 2 + 1) * CHUNKS + k
                            near = {"tensor": q - move if q != source else q + move}
                            piece = out.at[at, :]
                            if q != sink:
                                env.copy(piece, piece, sem, near).wait_send()
                            if q != source:
                                env.copy(piece, piece, back, near).wait_send()

                pl.when(env.place == q)(act)

        stages.append((1000, drain))
        return stages

    group.jobs.append(job)
    names = [n_out] + [n for n in (n_keep, n_sums) if n]
    return [n[1] for n in names]


def gather_line(group, piece):
    count, width = piece.shape
    places = lax.axis_size("tensor")
    if width % 128:
        return None
    group.peers.add("line")
    n_in = group.operand(piece, pltpu.VMEM)
    n_out = group.result((count, width * places), piece.dtype, pltpu.VMEM)
    base = group.sems(places)

    def job(env):
        source, out = env(n_in), env(n_out)

        def columns(index):
            return out.at[:, pl.ds(pl.multiple_of(index * width, width), width)]

        def begin():
            for j in sorted(range(1, places), key=lambda j: -min(j, places - j)):
                env.start(source, columns(env.place), base + j, env.along(j))
            env.local(source, columns(env.place), base)

        def end():
            for j in range(1, places):
                env.arrived(columns(lax.rem(env.place - j + places, places)), base + j)

        return [(-10, begin), (900, end)]

    group.jobs.append(job)
    return n_out[1]


def gather_all(group, piece):
    rows, width = piece.shape
    quads, places = lax.axis_size("seq"), lax.axis_size("tensor")
    group.peers.update(("plane", "line"))
    n_in = group.operand(piece, pltpu.VMEM)
    n_out = group.result((2, quads, places, rows, width), piece.dtype, pltpu.VMEM)
    base = group.sems(quads + places + 1)

    def job(env):
        source, out = env(n_in), env(n_out)
        mine = out.at[env.core, env.quad, env.place]

        def begin():
            mine[...] = source[...]
            for j in range(1, places):
                env.start(mine, mine, base + j, env.along(j))

        def second():
            for j in range(1, places):
                there = lax.rem(env.place - j + places, places)
                env.arrived(out.at[env.core, env.quad, there], base + j)
            line = out.at[env.core, env.quad]
            for j in range(1, quads):
                env.start(line, line, base + places + j, env.peer(j, 0))

        def third():
            for j in range(1, quads):
                there = lax.rem(env.quad - j + quads, quads)
                env.arrived(out.at[env.core, there], base + places + j)
            env.start(out.at[env.core], out.at[env.core], base, env.peer(0, 1))

        def end():
            env.arrived(out.at[1 - env.core], base)

        return [(-20, begin), (90, second), (91, third), (903, end)]

    group.jobs.append(job)
    return n_out[1]


def piece_of(ref, axis, slot, first, rows, shard, width):
    if axis == 0:
        return ref.at[pl.ds(pl.multiple_of(slot * shard + first, 16), rows), :]
    return ref.at[
        pl.ds(pl.multiple_of(first, 16), rows), pl.ds(pl.multiple_of(slot * width, width), width)
    ]


def gather_plane(group, layer, shard, axis, when):
    rows, width = shard.shape
    half = rows // 2
    quads = lax.axis_size("seq")
    group.peers.add("plane")
    full = (rows * quads, width) if axis == 0 else (rows, width * quads)
    n_in = group.operand(shard, pl.ANY)
    n_out = group.result(full, shard.dtype, pl.ANY)
    base = group.sems(3 * quads + 1)

    def job(env):
        source, out = env(n_in), env(n_out)
        holder = env.core == layer

        def part(slot, core):
            return piece_of(out, axis, slot, core * half, half, rows, width)

        def whole(slot):
            return piece_of(out, axis, slot, 0, rows, rows, width)

        def begin():
            for j in (2, 1, 3) if quads == 4 else range(1, quads):
                for flip in (0, 1):
                    core = abs(layer - flip)
                    env.start(
                        source.at[pl.ds(core * half, half), :], part(env.quad, core),
                        base + flip * quads + j, env.peer(j, flip), holder,
                    )
            env.start(source, whole(env.quad), base + quads, env.peer(0, 1), holder)
            env.local(source, whole(env.quad), base, holder)

        def pass_on():
            for j in range(1, quads):
                slot = lax.rem(env.quad - j + quads, quads)
                got = part(slot, env.core)

                @pl.when(holder)
                def _():
                    env.arrived(got, base + j)

                @pl.when(jnp.logical_not(holder))
                def _():
                    env.arrived(got, base + quads + j)

                env.start(got, got, base + 2 * quads + j, env.peer(0, 1))

        def end():
            for j in range(1, quads):
                slot = lax.rem(env.quad - j + quads, quads)
                env.arrived(part(slot, 1 - env.core), base + 2 * quads + j)

            @pl.when(jnp.logical_not(holder))
            def _():
                env.arrived(whole(env.quad), base + quads)

        return [(-5, begin), (when, pass_on), (901, end)]

    group.jobs.append(job)
    return n_out[1]


def reduce_plane(group, layer, grad, axis, times):
    quads = lax.axis_size("seq")
    rows = grad.shape[0] // quads if axis == 0 else grad.shape[0]
    width = grad.shape[1] if axis == 0 else grad.shape[1] // quads
    half = rows // 2
    step = 32
    group.peers.add("plane")
    n_in = group.operand(grad, pltpu.VMEM)
    n_out = group.result((rows, width), f32, pltpu.VMEM)
    n_land = group.room((quads, half, width), bf16)
    n_sum = group.room((quads, half, width), bf16)
    n_far = group.room((quads, half, width), bf16)
    n_fin = group.room((half, width), f32)
    base = group.sems(2 * quads + 1)

    def job(env):
        mine, out, land, total, far, fin = (
            env(n_in), env(n_out), env(n_land), env(n_sum), env(n_far), env(n_fin),
        )
        holder = env.core == layer
        order = [2, 1, 3, 0] if quads == 4 else list(range(1, quads)) + [0]

        def begin():
            for j in order:
                slot = lax.rem(env.quad + j, quads)
                env.start(
                    piece_of(mine, axis, slot, (1 - env.core) * half, half, rows, width),
                    land.at[slot], base + j, env.peer(0, 1),
                )

        def middle():
            for j in order:
                slot = lax.rem(env.quad + j, quads)
                env.arrived(land.at[slot], base + j)
                own = piece_of(mine, axis, slot, env.core * half, half, rows, width)

                def work(i, slot=slot, own=own):
                    at = pl.ds(i, step)
                    total[slot, at, :] = (
                        own[at, :].astype(f32) + land[slot, at, :].astype(f32)
                    ).astype(bf16)

                rows_loop(half, step, work)
                if j:
                    env.start(total.at[slot], far.at[j], base + quads + j, env.peer(j, 0))

        def close():
            for j in range(1, quads):
                env.arrived(far.at[j], base + quads + j)

            def work(i):
                at = pl.ds(i, step)
                value = total[env.quad, at, :].astype(f32)
                for j in range(1, quads):
                    value = value + far[j, at, :].astype(f32)
                fin[at, :] = value

            rows_loop(half, step, work)
            spot = out.at[pl.ds(pl.multiple_of(env.core * half, 16), half), :]
            env.start(fin, spot, base + 2 * quads, env.peer(0, 1), jnp.logical_not(holder))
            env.local(fin, spot, base + quads, holder)

        def end():
            @pl.when(holder)
            def _():
                spot = out.at[pl.ds(pl.multiple_of((1 - env.core) * half, 16), half), :]
                env.arrived(spot, base + 2 * quads)

        return [(-8, begin), (times[0], middle), (times[1], close), (902, end)]

    group.jobs.append(job)
    return n_out[1]


def sum_vectors(group, pair, shared):
    rows, width = pair.shape[1:]
    quads, places = lax.axis_size("seq"), lax.axis_size("tensor")
    group.peers.update(("plane", "line"))
    n_in = group.operand(pair, pltpu.VMEM)
    n_out = group.result((rows, width), f32, pltpu.VMEM)
    n_near = group.room((rows, width), f32)
    n_one = group.room((rows, width), f32)
    n_far = group.room((quads, rows, width), f32)
    n_two = group.room((rows, width), f32)
    n_end = group.room((places, rows, width), f32)
    base = group.sems(quads + places)

    def job(env):
        mine, out, near, one, far, two, ends = (
            env(n_in), env(n_out), env(n_near), env(n_one), env(n_far), env(n_two), env(n_end),
        )

        def go():
            env.start(mine.at[1 - env.core], near, base, env.peer(0, 1))
            env.arrived(near, base)
            one[...] = mine[env.core] + near[...]
            for j in range(1, quads):
                env.start(one, far.at[j], base + j, env.peer(j, 0))
            value = one[...]
            for j in range(1, quads):
                env.arrived(far.at[j], base + j)
                value = value + far[j]
            two[...] = value
            for j in range(1, places):
                env.start(two, ends.at[j], base + quads + j, env.along(j))
            for j in range(1, places):
                env.arrived(ends.at[j], base + quads + j)
                value = value + ends[j]
            row = lax.broadcasted_iota(jnp.int32, value.shape, 0)
            out[...] = jnp.where(row < shared, value, two[...])

        return [(0, go)]

    group.jobs.append(job)
    return n_out[1]


def allowed_mask(segment):
    length = segment.shape[1]
    place = lax.broadcasted_iota(jnp.int32, (length, length), 0)
    other = lax.broadcasted_iota(jnp.int32, (length, length), 1)
    same = segment[:, :, None] == segment[:, None, :]
    return (same & (other <= place)[None])[:, None]


def gelu_value(upper):
    return jax.nn.gelu(upper, approximate=True)


def dot(left, right, dims):
    return lax.dot_general(left, right, (dims, ((), ())), preferred_element_type=f32)


def attend(whole, mask, gain, bias, w_qkv, b_qv, w_out, heads):
    count = whole.shape[0]
    size = w_qkv.shape[1] // heads // 3
    shape4 = (mask.shape[0], mask.shape[2], heads, size)
    factor = 1.0 / math.sqrt(size)
    normed = (statistics(whole.astype(f32))[0] * gain + bias).astype(bf16)
    mixed = dot(normed, w_qkv, ((1,), (0,))).reshape(count, heads, 3 * size)
    query = (mixed[..., :size] + b_qv[:, :size]).astype(bf16).reshape(shape4)
    keys = mixed[..., size : 2 * size].astype(bf16).reshape(shape4)
    values = (mixed[..., 2 * size :] + b_qv[:, size:]).astype(bf16).reshape(shape4)
    scores = jnp.einsum("sqhe,skhe->shqk", query, keys, preferred_element_type=f32) * factor
    masked = jnp.where(mask, scores, floor_value)
    raised = jnp.exp(masked - jnp.max(masked, axis=-1, keepdims=True))
    chance = raised / jnp.sum(raised, axis=-1, keepdims=True)
    low = chance.astype(bf16)
    context = jnp.einsum("shqk,skhe->sqhe", low, values, preferred_element_type=f32)
    context = context.reshape(count, heads * size).astype(bf16)
    partial = dot(context, w_out, ((1,), (0,))).astype(bf16)
    return (partial, (normed, query, keys, values, chance, low, context))


def attend_back(whole_ga, kept, w_qkv, w_out):
    normed, query, keys, values, chance, low, context = kept
    count = whole_ga.shape[0]
    heads, size = query.shape[2:]
    factor = 1.0 / math.sqrt(size)
    grad_context = dot(whole_ga, w_out, ((1,), (1,))).astype(bf16).reshape(query.shape)
    grad_chance = jnp.einsum("sqhe,skhe->shqk", grad_context, values, preferred_element_type=f32)
    delta = jnp.sum(grad_chance * chance, axis=-1, keepdims=True)
    grad_scores = (chance * (grad_chance - delta)).astype(bf16)
    grad_query = (
        jnp.einsum("shqk,skhe->sqhe", grad_scores, keys, preferred_element_type=f32) * factor
    ).astype(bf16)
    grad_keys = (
        jnp.einsum("shqk,sqhe->skhe", grad_scores, query, preferred_element_type=f32) * factor
    ).astype(bf16)
    grad_values = jnp.einsum(
        "shqk,sqhe->skhe", low, grad_context, preferred_element_type=f32
    ).astype(bf16)
    grad_mixed = jnp.concatenate([grad_query, grad_keys, grad_values], axis=-1).reshape(
        count, heads * 3 * size
    )
    partial = dot(grad_mixed, w_qkv, ((1,), (1,))).astype(bf16)
    grad_out_w = dot(context, whole_ga, ((0,), (0,))).astype(bf16)
    grad_qkv = dot(normed, grad_mixed, ((0,), (0,))).astype(bf16)
    grad_qv = jnp.concatenate(
        [
            jnp.sum(grad_query.astype(f32), axis=(0, 1)),
            jnp.sum(grad_values.astype(f32), axis=(0, 1)),
        ],
        axis=-1,
    )
    return (partial, grad_out_w, grad_qkv, grad_qv)


def widen(normed2, w_up, b_up, w_down, last=True):
    upper = dot(normed2, w_up, ((1,), (0,))) + b_up
    active = gelu_value(upper).astype(bf16)
    partial = dot(active, w_down, ((1,), (0,))).astype(bf16)
    return (partial, (normed2, upper, active))


def widen_back(grad, kept, w_up, w_down):
    normed2, upper, active = kept
    grad_active = dot(grad, w_down, ((1,), (1,)))
    grad_upper = jax.vjp(gelu_value, upper)[1](grad_active)[0].astype(bf16)
    partial = dot(grad_upper, w_up, ((1,), (1,))).astype(bf16)
    grad_down = dot(active, grad, ((0,), (0,))).astype(bf16)
    grad_up = dot(normed2, grad_upper, ((0,), (0,))).astype(bf16)
    return (partial, grad_down, grad_up, jnp.sum(grad_upper.astype(f32), axis=0))


def swap(item):
    return lax.ppermute(item, "section", [(0, 1), (1, 0)])


def body(
    tokens, segments, cotangent, norm1_gain, norm1_bias, qkv_weight, qv_bias, out_weight, out_bias,
    norm2_gain, norm2_bias, up_weight, up_bias, down_weight, down_bias,
):
    section = lax.axis_index("section")
    place = lax.axis_index("tensor")
    quad = lax.axis_index("seq")
    tensors = lax.axis_size("tensor")
    quads = lax.axis_size("seq")
    first = section == 0
    rows_all, width = tokens.shape
    full = width * tensors
    heads, wide = qkv_weight.shape[2:]
    size = wide // 3
    part = norm1_gain.shape[1]
    part_up = up_bias.shape[1]
    part_qv = qv_bias.shape[2]
    hidden_units = up_weight.shape[2]

    def mine(item):
        return lax.dynamic_slice_in_dim(item, section * (item.shape[0] // 2), item.shape[0] // 2, 0)

    def columns_of(whole):
        return lax.dynamic_slice_in_dim(whole, place * width, width, 1)

    packed = jnp.concatenate(
        [
            norm1_gain[0], norm1_bias[0], out_bias[0], norm2_gain[0], norm2_bias[0], down_bias[0],
            up_bias[0], qv_bias[0].reshape(-1),
        ]
    )
    length = packed.shape[0]
    packed = jnp.pad(packed.astype(f32), (0, -length % 1024)).reshape(-1, 128)

    def vectors_of(layer):
        own = small[layer]
        vectors = [own[:, :, i * part : (i + 1) * part].reshape(1, full) for i in range(6)]
        local = lax.dynamic_slice_in_dim(own, place, 1, 0)[0]
        b_up = local[:, 6 * part : 6 * part + part_up].reshape(-1)
        b_qv = local[:, 6 * part + part_up :].reshape(quads, heads, part_qv)
        b_qv = jnp.transpose(b_qv, (1, 0, 2)).reshape(heads, 2 * size)
        return (vectors, b_up, b_qv)

    def block(*rows):
        return jnp.concatenate(
            list(rows) + [jnp.zeros((8 - len(rows), full), f32)], axis=0
        )

    shards = (
        (qkv_weight[0].reshape(-1, heads * wide), 0),
        (out_weight[0].reshape(heads * size, -1), 1),
        (up_weight[0], 0),
        (down_weight[0], 1),
    )
    mask = allowed_mask(mine(segments))

    def whole_of(index, item):
        if index is None:
            return lax.all_gather(mine(item), "tensor", axis=1, tiled=True)
        return got[index]

    start = Group(0)
    at_v = gather_all(start, packed)
    at_x = gather_line(start, mine(tokens))
    at_w = [gather_plane(start, 0, item, axis, 100 + i) for i, (item, axis) in enumerate(shards)]
    at_c = gather_line(start, mine(cotangent))
    got = start.run()
    small = jnp.transpose(got[at_v].reshape(2, quads, tensors, -1)[..., :length], (0, 2, 1, 3))
    whole0, cot = whole_of(at_x, tokens), whole_of(at_c, cotangent)
    weights0 = [got[i] for i in at_w]
    vec0, b_up0, b_qv0 = vectors_of(0)
    vec1, b_up1, b_qv1 = vectors_of(1)

    partial, kept_a0 = attend(whole0, mask, vec0[0], vec0[1], weights0[0], b_qv0, weights0[1], heads)
    call = Group(1)
    a = chain_sum(call, "f1", partial, block(vec0[2], vec0[3], vec0[4]), whole_in=whole0)
    at_w2 = [gather_plane(call, 1, *shards[i], when=6.5) for i in (2, 3)]
    got = call.run()
    normed2, hidden0 = got[a[0]], got[a[1]]
    up1, down1 = got[at_w2[0]], got[at_w2[1]]
    partial, kept_w0 = widen(normed2, weights0[2], b_up0, weights0[3])
    call = Group(2)
    a = chain_sum(call, "f2", partial, block(vec0[5]), half_in=hidden0)
    at_w2 = [gather_plane(call, 1, *shards[i], when=5.5) for i in (0, 1)]
    got = call.run()
    whole1 = got[a[0]]
    qkv1, out1 = got[at_w2[0]], got[at_w2[1]]

    partial, kept_a1 = attend(whole1, mask, vec1[0], vec1[1], qkv1, b_qv1, out1, heads)
    call = Group(3)
    a = chain_sum(call, "f1", partial, block(vec1[2], vec1[3], vec1[4]), whole_in=whole1)
    got = call.run()
    normed2, hidden1 = got[a[0]], got[a[1]]
    partial, kept_w1 = widen(normed2, up1, b_up1, down1)
    call = Group(4)
    a = chain_sum(call, "f2", partial, block(vec1[5]), half_in=hidden1)
    whole2 = call.run()[a[0]]

    partial, g_down1, g_up1, s_up1 = widen_back(cot, kept_w1, up1, down1)
    call = Group(5)
    a = chain_sum(call, "b1", partial, block(vec1[3]), whole_in=cot, half_in=hidden1)
    at_g = [
        reduce_plane(call, 1, g_up1, 0, (1.5, 8.5)), reduce_plane(call, 1, g_down1, 1, (2.5, 9.5))
    ]
    got = call.run()
    ga, dhidden, sums_b1 = got[a[0]], got[a[1]], got[a[2]]
    r_up1, r_down1 = got[at_g[0]], got[at_g[1]]
    partial, g_out1, g_qkv1, s_qv1 = attend_back(ga, kept_a1, qkv1, out1)
    call = Group(6)
    a = chain_sum(call, "b2", partial, block(vec1[0]), whole_in=whole1, half_in=dhidden)
    at_g = [
        reduce_plane(call, 1, g_qkv1, 0, (1.5, 7.5)), reduce_plane(call, 1, g_out1, 1, (1.6, 7.6))
    ]
    got = call.run()
    grad1, sums_b2 = got[a[0]], got[a[1]]
    r_qkv1, r_out1 = got[at_g[0]], got[at_g[1]]

    partial, g_down0, g_up0, s_up0 = widen_back(grad1, kept_w0, weights0[2], weights0[3])
    call = Group(7)
    a = chain_sum(call, "b1", partial, block(vec0[3]), whole_in=grad1, half_in=hidden0)
    at_g = [
        reduce_plane(call, 0, g_up0, 0, (1.5, 8.5)), reduce_plane(call, 0, g_down0, 1, (2.5, 9.5))
    ]
    got = call.run()
    ga, dhidden, sums_a1 = got[a[0]], got[a[1]], got[a[2]]
    r_up0, r_down0 = got[at_g[0]], got[at_g[1]]
    partial, g_out0, g_qkv0, s_qv0 = attend_back(ga, kept_a0, weights0[0], weights0[1])
    call = Group(8)
    a = chain_sum(call, "b2", partial, block(vec0[0]), whole_in=whole0, half_in=dhidden)
    at_g = [
        reduce_plane(call, 0, g_qkv0, 0, (1.5, 7.5)), reduce_plane(call, 0, g_out0, 1, (1.6, 7.6))
    ]
    got = call.run()
    grad0, sums_a2 = got[a[0]], got[a[1]]
    r_qkv0, r_out0 = got[at_g[0]], got[at_g[1]]

    def rows_of(sums_one, sums_two, up, qv):
        one = jnp.sum(sums_one.reshape(4, 8, full), axis=1)
        two = jnp.sum(sums_two.reshape(2, 8, full), axis=1)
        flat = [
            jnp.pad(item.reshape(1, -1), ((0, 0), (0, full - item.size))) for item in (up, qv)
        ]
        return jnp.concatenate(
            [two[0:1], two[1:2], one[2:3], one[0:1], one[1:2], one[3:4]] + flat, axis=0
        )

    call = Group(9)
    a = sum_vectors(
        call, jnp.stack([rows_of(sums_a1, sums_a2, s_up0, s_qv0), rows_of(sums_b1, sums_b2, s_up1, s_qv1)]), 6
    )
    vectors = call.run()[a]
    spot = (place * quads + quad) * part
    small_grads = [lax.dynamic_slice(vectors, (i, spot), (1, part))[0] for i in range(6)]
    g_up = lax.dynamic_slice(vectors, (6, quad * part_up), (1, part_up))[0]
    g_qv = vectors[7, : heads * 2 * size].reshape(heads, quads, part_qv)
    g_qv = lax.dynamic_slice_in_dim(g_qv, quad, 1, 1)[:, 0]

    def settle(of0, of1):
        of0, of1 = columns_of(of0), columns_of(of1)
        own = jnp.where(first, of0, of1)
        other = swap(jnp.where(first, of1, of0))
        return jnp.where(
            first, jnp.concatenate([own, other]), jnp.concatenate([other, own])
        )

    outputs = settle(whole1, whole2)
    input_grads = settle(grad0, grad1)
    totals = [
        jnp.where(first, one, two)
        for one, two in ((r_qkv0, r_qkv1), (r_out0, r_out1), (r_up0, r_up1), (r_down0, r_down1))
    ]
    result = (
        outputs,
        input_grads,
        small_grads[0],
        small_grads[1],
        totals[0].reshape(-1, heads, wide),
        g_qv,
        totals[1].reshape(heads, size, -1),
        small_grads[2],
        small_grads[3],
        small_grads[4],
        totals[2],
        g_up,
        totals[3],
        small_grads[5],
    )
    return tuple(item[None] for item in result)


def solution(mesh):
    vector = P("section", ("tensor", "seq"))
    return jax.shard_map(
        body,
        mesh=mesh,
        in_specs=(
            P("seq", "tensor"),
            P("seq", None),
            P("seq", "tensor"),
            vector,
            vector,
            P("section", "seq", "tensor", None),
            P("section", "tensor", "seq"),
            P("section", "tensor", None, "seq"),
            vector,
            vector,
            vector,
            P("section", "seq", "tensor"),
            vector,
            P("section", "tensor", "seq"),
            vector,
        ),
        out_specs=(
            P("section", "seq", "tensor"),
            P("section", "seq", "tensor"),
            vector,
            vector,
            P("section", "seq", "tensor", None),
            P("section", "tensor", "seq"),
            P("section", "tensor", None, "seq"),
            vector,
            vector,
            vector,
            P("section", "seq", "tensor"),
            vector,
            P("section", "tensor", "seq"),
            vector,
        ),
        check_vma=False,
    )
```

```python
import math

import jax
import jax.numpy as jnp
from jax import lax
from jax.experimental import pallas as pl
from jax.experimental.pallas import tpu as pltpu
from jax.sharding import PartitionSpec as P

epsilon = 1e-05
floor_value = -1e30
f32 = jnp.float32
bf16 = jnp.bfloat16
MESH = pl.DeviceIdType.MESH
CHUNKS = 4
STEP = 16
TILE = 256
root = math.sqrt(2.0 / math.pi)
cubic = 0.044715


class Group:
    def __init__(self, number):
        self.number = number
        self.ins, self.in_specs = [], []
        self.outs, self.out_specs = [], []
        self.scratch = []
        self.count = 0
        self.jobs = []
        self.peers = set()
        self.ticks = 0

    def operand(self, value, space):
        self.ins.append(value)
        self.in_specs.append(pl.BlockSpec(memory_space=space))
        return ("in", len(self.ins) - 1)

    def result(self, shape, dtype, space):
        self.outs.append(jax.ShapeDtypeStruct(shape, dtype))
        self.out_specs.append(pl.BlockSpec(memory_space=space))
        return ("out", len(self.outs) - 1)

    def room(self, shape, dtype):
        self.scratch.append(pltpu.VMEM(shape, dtype))
        return ("tmp", len(self.scratch) - 1)

    def scratch_shape(self, name):
        return self.scratch[name[1]].shape

    def sems(self, count):
        first = self.count
        self.count += count
        return first

    def run(self):
        n_in, n_out, n_tmp = len(self.ins), len(self.outs), len(self.scratch)

        def kernel(*refs):
            banks = {
                "in": refs[:n_in],
                "out": refs[n_in : n_in + n_out],
                "tmp": refs[n_in + n_out : n_in + n_out + n_tmp],
            }
            env = Env(banks, refs[-2], refs[-1])
            env.greet(self.peers)
            stages = []
            for job in self.jobs:
                stages.extend(job(env))
            stages.sort(key=lambda item: item[0])
            for when, stage in stages:
                if when < 0:
                    stage()
            timed = [item for item in stages if 0 <= item[0] < self.ticks]

            def one(tick, carry):
                for tick_of in env.looped:
                    tick_of(tick)
                for when, stage in timed:
                    pl.when(tick == when)(stage)
                return carry

            if self.ticks:
                lax.fori_loop(0, self.ticks, one, 0)
            for when, stage in stages:
                if when >= self.ticks:
                    stage()
            env.finish()

        return pl.pallas_call(
            kernel,
            out_shape=tuple(self.outs),
            in_specs=self.in_specs,
            out_specs=tuple(self.out_specs),
            scratch_shapes=self.scratch
            + [pltpu.SemaphoreType.DMA((self.count,)), pltpu.SemaphoreType.DMA((self.count,))],
            compiler_params=pltpu.CompilerParams(
                collective_id=self.number, has_side_effects=True, vmem_limit_bytes=48 << 20
            ),
        )(*self.ins)


class Env:
    def __init__(self, banks, send, recv):
        self.banks, self.send, self.recv = banks, send, recv
        self.core = lax.axis_index("section")
        self.quad = lax.axis_index("seq")
        self.place = lax.axis_index("tensor")
        self.cores = lax.axis_size("section")
        self.quads = lax.axis_size("seq")
        self.places = lax.axis_size("tensor")
        self.pending = []
        self.looped = []
        self.peers = [[self.reach(j, flip) for flip in (0, 1)] for j in range(self.quads)]
        self.line = [{"tensor": lax.rem(self.place + j, self.places)} for j in range(self.places)]
        self.other = 1 - self.core

    def __call__(self, name):
        return self.banks[name[0]][name[1]]

    def greet(self, peers):
        barrier = pltpu.get_barrier_semaphore()
        total = 0
        if "plane" in peers:
            for core in range(2):
                for j in range(self.quads):
                    if core == 0 and j == 0:
                        continue
                    pl.semaphore_signal(
                        barrier, inc=1, device_id=self.peer(j, core), device_id_type=MESH
                    )
                    total += 1
        if "line" in peers:
            for j in range(1, self.places):
                pl.semaphore_signal(barrier, inc=1, device_id=self.along(j), device_id_type=MESH)
                total += 1
        elif "next" in peers:
            for shift in (-1, 1):
                there = self.place + shift

                @pl.when((there >= 0) & (there < self.places))
                def _():
                    pl.semaphore_signal(
                        barrier, inc=1, device_id={"tensor": there}, device_id_type=MESH
                    )

            edge = (self.place == 0) | (self.place == self.places - 1)
            amount = total

            @pl.when(edge)
            def _():
                pl.semaphore_wait(barrier, amount + 1)

            @pl.when(jnp.logical_not(edge))
            def _():
                pl.semaphore_wait(barrier, amount + 2)

            return
        pl.semaphore_wait(barrier, total)

    def peer(self, j, flip):
        return self.peers[j][flip]

    def along(self, j):
        return self.line[j]

    def reach(self, j, flip):
        target = {"seq": lax.rem(self.quad + j, self.quads)}
        target["section"] = (1 - self.core) if flip else self.core
        return target

    def copy(self, source, target, sem, device):
        return pltpu.make_async_remote_copy(
            src_ref=source,
            dst_ref=target,
            send_sem=self.send.at[sem],
            recv_sem=self.recv.at[sem],
            device_id=device,
            device_id_type=MESH,
        )

    def start(self, source, target, sem, device, when=None):
        made = self.copy(source, target, sem, device)
        if when is None:
            made.start()
        else:
            pl.when(when)(made.start)
        self.pending.append((lambda: self.copy(source, target, sem, device).wait_send(), when))

    def arrived(self, target, sem):
        self.copy(target, target, sem, {"section": 1 - self.core}).wait_recv()

    def local(self, source, target, sem, when=None):
        made = pltpu.make_async_copy(source, target, self.send.at[sem])
        if when is None:
            made.start()
        else:
            pl.when(when)(made.start)
        self.pending.append(
            (lambda: pltpu.make_async_copy(source, target, self.send.at[sem]).wait(), when)
        )

    def finish(self):
        for wait, when in self.pending:
            if when is None:
                wait()
            else:
                pl.when(when)(wait)


def rows_loop(count, step, work):
    def one(i, carry):
        work(pl.multiple_of(i * step, step))
        return carry

    lax.fori_loop(0, count // step, one, 0)


def statistics(rows):
    average = jnp.mean(rows, axis=1, keepdims=True)
    variance = jnp.mean(rows * rows, axis=1, keepdims=True) - average * average
    scale = lax.rsqrt(variance + epsilon)
    return ((rows - average) * scale, scale)


def norm_backward(grad, centred, scale, gain):
    scaled = grad * gain
    total = jnp.mean(scaled, axis=1, keepdims=True)
    along = jnp.mean(scaled * centred, axis=1, keepdims=True)
    return scale * (scaled - total - centred * along)


def name_of(group, value):
    return value if isinstance(value, tuple) else group.operand(value, pltpu.VMEM)


def chain_sum(group, kind, part, vectors, flip=False, start=0, produce=None, wide=None, kept=None):
    if produce is None:
        count, width = part.shape
    else:
        count, width = group.scratch_shape(part)
    half = count // 2
    chunk = half // CHUNKS
    group.peers.add("next")
    n_part = name_of(group, part)
    n_vec = name_of(group, vectors) if vectors is not None else None
    n_wide = name_of(group, wide) if wide is not None else None
    n_half = name_of(group, kept) if kept is not None else None
    n_out = group.result((count, width), bf16, pltpu.VMEM)
    n_keep = group.result((half, width), f32, pltpu.VMEM) if kind in ("f1", "b1") else None
    sums = {"f1": 0, "f2": 0, "b1": 4, "b2": 2}[kind]
    n_sums = group.result((sums * 8, width), f32, pltpu.VMEM) if sums else None
    n_land = group.room((2, half, width), bf16)
    n_go = group.room((2, half, width), bf16)
    base = group.sems(4 * CHUNKS)
    last = lax.axis_size("tensor") - 1
    group.ticks = max(group.ticks, start + CHUNKS + 2 * last)

    def job(env):
        part, out, land, go = env(n_part), env(n_out), env(n_land), env(n_go)
        vec = env(n_vec) if n_vec else None
        wide = env(n_wide) if n_wide else None
        kept = env(n_half) if n_half else None
        keep = env(n_keep) if n_keep else None
        acc = env(n_sums) if n_sums else None

        def prepare():
            if acc is not None:
                acc[...] = jnp.zeros_like(acc)
            if keep is not None:
                keep[...] = jnp.zeros_like(keep)

        def add(row, value):
            acc[row * 8 : row * 8 + 8, :] += jnp.sum(
                value.reshape(STEP // 8, 8, width), axis=0
            )

        def close(side, k):
            def work(i):
                own = pl.ds(pl.multiple_of(k * chunk + i, STEP), STEP)
                at = pl.ds(pl.multiple_of(side * half + k * chunk + i, STEP), STEP)
                total = land[side, own, :].astype(f32) + part[at, :].astype(f32)
                if kind == "f1":
                    hidden = wide[at, :].astype(f32) + (total + vec[0:1, :])
                    keep[own, :] = hidden
                    centred, _ = statistics(hidden)
                    out[at, :] = (centred * vec[1:2, :] + vec[2:3, :]).astype(bf16)
                elif kind == "f2":
                    out[at, :] = total.astype(bf16)
                elif kind == "b1":
                    centred, scale = statistics(kept[own, :])
                    upstream = wide[at, :].astype(f32)
                    grad = upstream + norm_backward(total, centred, scale, vec[0:1, :])
                    keep[own, :] = grad
                    low = grad.astype(bf16)
                    out[at, :] = low
                    add(0, total * centred)
                    add(1, total)
                    add(2, low.astype(f32))
                    add(3, upstream)
                else:
                    centred, scale = statistics(wide[at, :].astype(f32))
                    grad = kept[own, :] + norm_backward(total, centred, scale, vec[0:1, :])
                    out[at, :] = grad.astype(bf16)
                    add(0, total * centred)
                    add(1, total)

            rows_loop(chunk, STEP, work)

        def layout(side):
            right = (side == 0) != flip
            steps = env.place if right else last - env.place
            there = env.place + 1 if right else env.place - 1
            back = env.place - 1 if right else env.place + 1
            return (
                steps, {"tensor": there}, {"tensor": back},
                base + 2 * side * CHUNKS, base + (2 * side + 1) * CHUNKS,
            )

        def slices(side, k):
            at = pl.ds(pl.multiple_of(side * half + k * chunk, STEP), chunk)
            own = pl.ds(pl.multiple_of(k * chunk, STEP), chunk)
            return at, own

        def due(k):
            return (k >= 0) & (k < CHUNKS)

        def forward(tick, side):
            steps, there, back, sem, sem_back = layout(side)
            k = tick - start - steps

            @pl.when(due(k))
            def _():
                at, own = slices(side, k)
                if produce is not None:
                    produce(env, side, k, at, own, steps == 0)

                @pl.when(steps > 0)
                def _():
                    env.arrived(land.at[side, own, :], sem + k)

                @pl.when(steps == last)
                def _():
                    close(side, k)
                    env.copy(out.at[at, :], out.at[at, :], sem_back + k, back).start()

                @pl.when(steps == 0)
                def _():
                    env.copy(part.at[at, :], land.at[side, own, :], sem + k, there).start()

                @pl.when((steps > 0) & (steps < last))
                def _():
                    def work(i):
                        i_own = pl.ds(pl.multiple_of(k * chunk + i, STEP), STEP)
                        i_at = pl.ds(pl.multiple_of(side * half + k * chunk + i, STEP), STEP)
                        go[side, i_own, :] = (
                            land[side, i_own, :].astype(f32) + part[i_at, :].astype(f32)
                        ).astype(bf16)

                    rows_loop(chunk, STEP, work)
                    env.copy(go.at[side, own, :], land.at[side, own, :], sem + k, there).start()

        def backward(tick, side):
            steps, there, back, sem, sem_back = layout(side)
            k = tick - start - (2 * last - steps)

            @pl.when(due(k) & (steps < last))
            def _():
                at, own = slices(side, k)
                env.arrived(out.at[at, :], sem_back + k)

                @pl.when(steps > 0)
                def _():
                    env.copy(out.at[at, :], out.at[at, :], sem_back + k, back).start()

        def tick_of(tick):
            for side in (0, 1):
                forward(tick, side)
            for side in (0, 1):
                backward(tick, side)

        def drain():
            for side in (0, 1):
                steps, there, back, sem, sem_back = layout(side)

                def one(k, carry, side=side, steps=steps, sem=sem, sem_back=sem_back):
                    at, own = slices(side, k)
                    piece = out.at[at, :]
                    near = {"section": 1 - env.core}

                    @pl.when(steps < last)
                    def _():
                        env.copy(piece, piece, sem + k, near).wait_send()

                    @pl.when(steps > 0)
                    def _():
                        env.copy(piece, piece, sem_back + k, near).wait_send()

                    return carry

                lax.fori_loop(0, CHUNKS, one, 0)

        env.looped.append(tick_of)
        return [(-30, prepare), (2000, drain)]

    group.jobs.append(job)
    return n_out, n_keep, n_sums


def column_loop(count, tile, work):
    def one(j, carry):
        work(pl.ds(pl.multiple_of(j * tile, tile), tile))
        return carry

    lax.fori_loop(0, count // tile, one, 0)


def feed_forward(source, kept, vectors, up, down, b_up, upper, active, part):
    def produce(env, side, k, at, own, first):
        rows, residual, vec, w_up, w_down = (
            env(source), env(kept), env(vectors), env(up), env(down),
        )
        bias, o_upper, o_active, o_part = env(b_up), env(upper), env(active), env(part)
        units, width = w_down.shape

        def widen(cols):
            value = dot(rows[at, :], w_up[:, cols], ((1,), (0,))) + bias[0:1, cols]
            o_upper[at, cols] = value
            bent = jnp.tanh(root * (value + cubic * (value * value * value)))
            o_active[at, cols] = (0.5 * value * (1.0 + bent)).astype(bf16)

        def narrow(cols):
            value = dot(o_active[at, :], w_down[:, cols], ((1,), (0,)))
            extra = jnp.where(first, residual[own, cols] + vec[5:6, cols], 0.0)
            o_part[at, cols] = (value + extra).astype(bf16)

        column_loop(units, min(TILE, units), widen)
        column_loop(width, TILE, narrow)

    return produce


def feed_back(source, up, down, upper, grad_upper, part):
    def produce(env, side, k, at, own, first):
        rows, w_up, w_down = env(source), env(up), env(down)
        i_upper, o_grad, o_part = env(upper), env(grad_upper), env(part)
        units, width = w_down.shape

        def widen(cols):
            value = i_upper[at, cols]
            square = value * value
            bent = jnp.tanh(root * (value + cubic * (value * square)))
            slope = 0.5 * (1.0 + bent) + 0.5 * value * (1.0 - bent * bent) * (
                root * (1.0 + 3.0 * cubic * square)
            )
            grad = dot(rows[at, :], w_down[cols, :], ((1,), (1,)))
            o_grad[at, cols] = (grad * slope).astype(bf16)

        def narrow(cols):
            value = dot(o_grad[at, :], w_up[cols, :], ((1,), (1,)))
            o_part[at, cols] = value.astype(bf16)

        column_loop(units, min(TILE, units), widen)
        column_loop(width, TILE, narrow)

    return produce


def gather_line(group, piece):
    count, width = piece.shape
    places = lax.axis_size("tensor")
    if width % 128:
        return None
    group.peers.add("line")
    n_in = group.operand(piece, pltpu.VMEM)
    n_out = group.result((count, width * places), piece.dtype, pltpu.VMEM)
    base = group.sems(places)

    def job(env):
        source, out = env(n_in), env(n_out)

        def columns(index):
            return out.at[:, pl.ds(pl.multiple_of(index * width, width), width)]

        def begin():
            for j in sorted(range(1, places), key=lambda j: -min(j, places - j)):
                env.start(source, columns(env.place), base + j, env.along(j))
            env.local(source, columns(env.place), base)

        def end():
            for j in range(1, places):
                env.arrived(columns(lax.rem(env.place - j + places, places)), base + j)

        return [(-10, begin), (900, end)]

    group.jobs.append(job)
    return n_out[1]


def gather_all(group, piece):
    rows, width = piece.shape
    quads, places = lax.axis_size("seq"), lax.axis_size("tensor")
    group.peers.update(("plane", "line"))
    n_in = group.operand(piece, pltpu.VMEM)
    n_out = group.result((2, quads, places, rows, width), piece.dtype, pltpu.VMEM)
    base = group.sems(quads + places + 1)

    def job(env):
        source, out = env(n_in), env(n_out)
        mine = out.at[env.core, env.quad, env.place]

        def begin():
            mine[...] = source[...]
            for j in range(1, places):
                env.start(mine, mine, base + j, env.along(j))

        def second():
            for j in range(1, places):
                there = lax.rem(env.place - j + places, places)
                env.arrived(out.at[env.core, env.quad, there], base + j)
            line = out.at[env.core, env.quad]
            for j in range(1, quads):
                env.start(line, line, base + places + j, env.peer(j, 0))

        def third():
            for j in range(1, quads):
                there = lax.rem(env.quad - j + quads, quads)
                env.arrived(out.at[env.core, there], base + places + j)
            env.start(out.at[env.core], out.at[env.core], base, env.peer(0, 1))

        def end():
            env.arrived(out.at[1 - env.core], base)

        return [(-20, begin), (90, second), (91, third), (903, end)]

    group.jobs.append(job)
    return n_out[1]


def piece_of(ref, axis, slot, first, rows, shard, width):
    if axis == 0:
        return ref.at[pl.ds(pl.multiple_of(slot * shard + first, 16), rows), :]
    if not isinstance(first, int):
        first = pl.multiple_of(first, 16)
    return ref.at[
        pl.ds(first, rows), pl.ds(pl.multiple_of(slot * width, width), width)
    ]


def gather_plane(group, layer, shard, axis, when):
    rows, width = shard.shape
    half = rows // 2
    quads = lax.axis_size("seq")
    group.peers.add("plane")
    full = (rows * quads, width) if axis == 0 else (rows, width * quads)
    n_in = group.operand(shard, pl.ANY)
    n_out = group.result(full, shard.dtype, pl.ANY)
    base = group.sems(3 * quads + 1)

    def job(env):
        source, out = env(n_in), env(n_out)
        holder = env.core == layer

        def part(slot, core):
            return piece_of(out, axis, slot, core * half, half, rows, width)

        def whole(slot):
            return piece_of(out, axis, slot, 0, rows, rows, width)

        other = jnp.logical_not(holder)
        slots = [lax.rem(env.quad - j + quads, quads) for j in range(quads)]
        mine = [part(slot, env.core) for slot in slots]
        theirs = [part(slot, env.other) for slot in slots]

        def begin():
            for j in (2, 1, 3) if quads == 4 else range(1, quads):
                for flip in (0, 1):
                    core = abs(layer - flip)
                    env.start(
                        source.at[pl.ds(core * half, half), :], part(env.quad, core),
                        base + flip * quads + j, env.peer(j, flip), holder,
                    )
            env.start(source, whole(env.quad), base + quads, env.peer(0, 1), holder)
            env.local(source, whole(env.quad), base, holder)

        def pass_on():
            for j in range(1, quads):
                got = mine[j]

                @pl.when(holder)
                def _():
                    env.arrived(got, base + j)

                @pl.when(other)
                def _():
                    env.arrived(got, base + quads + j)

                env.start(got, got, base + 2 * quads + j, env.peer(0, 1))

        def end():
            for j in range(1, quads):
                env.arrived(theirs[j], base + 2 * quads + j)

            @pl.when(other)
            def _():
                env.arrived(whole(env.quad), base + quads)

        return [(-5, begin), (when, pass_on), (901, end)]

    group.jobs.append(job)
    return n_out[1]


def reduce_plane(group, layer, grad, axis, times):
    quads = lax.axis_size("seq")
    rows = grad.shape[0] // quads if axis == 0 else grad.shape[0]
    width = grad.shape[1] if axis == 0 else grad.shape[1] // quads
    half = rows // 2
    step = 32
    group.peers.add("plane")
    n_in = group.operand(grad, pltpu.VMEM)
    n_out = group.result((rows, width), f32, pltpu.VMEM)
    n_land = group.room((quads, half, width), bf16)
    n_sum = group.room((quads, half, width), bf16)
    n_far = group.room((quads, half, width), bf16)
    n_fin = group.room((half, width), f32)
    base = group.sems(2 * quads + 1)

    def job(env):
        mine, out, land, total, far, fin = (
            env(n_in), env(n_out), env(n_land), env(n_sum), env(n_far), env(n_fin),
        )
        holder = env.core == layer
        other = jnp.logical_not(holder)
        order = [2, 1, 3, 0] if quads == 4 else list(range(1, quads)) + [0]
        slots = [lax.rem(env.quad + j, quads) for j in range(quads)]
        mine_of = [
            piece_of(mine, axis, slot, env.core * half, half, rows, width) for slot in slots
        ]
        their_of = [
            piece_of(mine, axis, slot, env.other * half, half, rows, width) for slot in slots
        ]
        lands = [land.at[slot] for slot in slots]
        totals = [total.at[slot] for slot in slots]
        fars = [far.at[lax.rem(env.quad, 1) + j] for j in range(quads)]
        spot_mine = out.at[pl.ds(pl.multiple_of(env.core * half, 16), half), :]
        spot_other = out.at[pl.ds(pl.multiple_of(env.other * half, 16), half), :]

        def begin():
            for j in order:
                env.start(their_of[j], lands[j], base + j, env.peer(0, 1))

        def middle():
            for j in order:
                slot = slots[j]
                env.arrived(lands[j], base + j)
                own = mine_of[j]

                def work(i, slot=slot, own=own):
                    at = pl.ds(i, step)
                    total[slot, at, :] = (
                        own[at, :].astype(f32) + land[slot, at, :].astype(f32)
                    ).astype(bf16)

                rows_loop(half, step, work)
                if j:
                    env.start(totals[j], fars[j], base + quads + j, env.peer(j, 0))

        def close():
            for j in range(1, quads):
                env.arrived(far.at[j], base + quads + j)

            def work(i):
                at = pl.ds(i, step)
                value = total[env.quad, at, :].astype(f32)
                for j in range(1, quads):
                    value = value + far[j, at, :].astype(f32)
                fin[at, :] = value

            rows_loop(half, step, work)
            env.start(fin, spot_mine, base + 2 * quads, env.peer(0, 1), other)
            env.local(fin, spot_mine, base + quads, holder)

        def end():
            @pl.when(holder)
            def _():
                env.arrived(spot_other, base + 2 * quads)

        return [(-8, begin), (times[0], middle), (times[1], close), (902, end)]

    group.jobs.append(job)
    return n_out[1]


def sum_vectors(group, pair, shared):
    rows, width = pair.shape[1:]
    quads, places = lax.axis_size("seq"), lax.axis_size("tensor")
    group.peers.update(("plane", "line"))
    n_in = group.operand(pair, pltpu.VMEM)
    n_out = group.result((rows, width), f32, pltpu.VMEM)
    n_near = group.room((rows, width), f32)
    n_one = group.room((rows, width), f32)
    n_far = group.room((quads, rows, width), f32)
    n_two = group.room((rows, width), f32)
    n_end = group.room((places, rows, width), f32)
    base = group.sems(quads + places)

    def job(env):
        mine, out, near, one, far, two, ends = (
            env(n_in), env(n_out), env(n_near), env(n_one), env(n_far), env(n_two), env(n_end),
        )

        def go():
            env.start(mine.at[1 - env.core], near, base, env.peer(0, 1))
            env.arrived(near, base)
            one[...] = mine[env.core] + near[...]
            for j in range(1, quads):
                env.start(one, far.at[j], base + j, env.peer(j, 0))
            value = one[...]
            for j in range(1, quads):
                env.arrived(far.at[j], base + j)
                value = value + far[j]
            two[...] = value
            for j in range(1, places):
                env.start(two, ends.at[j], base + quads + j, env.along(j))
            for j in range(1, places):
                env.arrived(ends.at[j], base + quads + j)
                value = value + ends[j]
            row = lax.broadcasted_iota(jnp.int32, value.shape, 0)
            out[...] = jnp.where(row < shared, value, two[...])

        return [(0, go)]

    group.jobs.append(job)
    return n_out[1]


def allowed_mask(segment):
    length = segment.shape[1]
    place = lax.broadcasted_iota(jnp.int32, (length, length), 0)
    other = lax.broadcasted_iota(jnp.int32, (length, length), 1)
    same = segment[:, :, None] == segment[:, None, :]
    return (same & (other <= place)[None])[:, None]


def dot(left, right, dims):
    return lax.dot_general(left, right, (dims, ((), ())), preferred_element_type=f32)


def attend(whole, mask, gain, bias, w_qkv, b_qv, w_out, heads):
    count = whole.shape[0]
    size = w_qkv.shape[1] // heads // 3
    shape4 = (mask.shape[0], mask.shape[2], heads, size)
    factor = 1.0 / math.sqrt(size)
    normed = (statistics(whole.astype(f32))[0] * gain + bias).astype(bf16)
    mixed = dot(normed, w_qkv, ((1,), (0,))).reshape(count, heads, 3 * size)
    query = (mixed[..., :size] + b_qv[:, :size]).astype(bf16).reshape(shape4)
    keys = mixed[..., size : 2 * size].astype(bf16).reshape(shape4)
    values = (mixed[..., 2 * size :] + b_qv[:, size:]).astype(bf16).reshape(shape4)
    scores = jnp.einsum("sqhe,skhe->shqk", query, keys, preferred_element_type=f32) * factor
    masked = jnp.where(mask, scores, floor_value)
    raised = jnp.exp(masked - jnp.max(masked, axis=-1, keepdims=True))
    chance = raised / jnp.sum(raised, axis=-1, keepdims=True)
    low = chance.astype(bf16)
    context = jnp.einsum("shqk,skhe->sqhe", low, values, preferred_element_type=f32)
    context = context.reshape(count, heads * size).astype(bf16)
    partial = dot(context, w_out, ((1,), (0,))).astype(bf16)
    return (partial, (normed, query, keys, values, chance, low, context))


def attend_back(whole_ga, kept, w_qkv, w_out):
    normed, query, keys, values, chance, low, context = kept
    count = whole_ga.shape[0]
    heads, size = query.shape[2:]
    factor = 1.0 / math.sqrt(size)
    grad_context = dot(whole_ga, w_out, ((1,), (1,))).astype(bf16).reshape(query.shape)
    grad_chance = jnp.einsum("sqhe,skhe->shqk", grad_context, values, preferred_element_type=f32)
    delta = jnp.sum(grad_chance * chance, axis=-1, keepdims=True)
    grad_scores = (chance * (grad_chance - delta)).astype(bf16)
    grad_query = (
        jnp.einsum("shqk,skhe->sqhe", grad_scores, keys, preferred_element_type=f32) * factor
    ).astype(bf16)
    grad_keys = (
        jnp.einsum("shqk,sqhe->skhe", grad_scores, query, preferred_element_type=f32) * factor
    ).astype(bf16)
    grad_values = jnp.einsum(
        "shqk,sqhe->skhe", low, grad_context, preferred_element_type=f32
    ).astype(bf16)
    grad_mixed = jnp.concatenate([grad_query, grad_keys, grad_values], axis=-1).reshape(
        count, heads * 3 * size
    )
    partial = dot(grad_mixed, w_qkv, ((1,), (1,))).astype(bf16)
    grad_out_w = dot(context, whole_ga, ((0,), (0,))).astype(bf16)
    grad_qkv = dot(normed, grad_mixed, ((0,), (0,))).astype(bf16)
    grad_qv = jnp.concatenate(
        [
            jnp.sum(grad_query.astype(f32), axis=(0, 1)),
            jnp.sum(grad_values.astype(f32), axis=(0, 1)),
        ],
        axis=-1,
    )
    return (partial, grad_out_w, grad_qkv, grad_qv)


def swap(item):
    return lax.ppermute(item, "section", [(0, 1), (1, 0)])


def body(
    tokens, segments, cotangent, norm1_gain, norm1_bias, qkv_weight, qv_bias, out_weight, out_bias,
    norm2_gain, norm2_bias, up_weight, up_bias, down_weight, down_bias,
):
    section = lax.axis_index("section")
    place = lax.axis_index("tensor")
    quad = lax.axis_index("seq")
    tensors = lax.axis_size("tensor")
    quads = lax.axis_size("seq")
    first = section == 0
    rows_all, width = tokens.shape
    full = width * tensors
    heads, wide = qkv_weight.shape[2:]
    size = wide // 3
    part = norm1_gain.shape[1]
    part_up = up_bias.shape[1]
    part_qv = qv_bias.shape[2]
    hidden_units = up_weight.shape[2]

    def mine(item):
        return lax.dynamic_slice_in_dim(item, section * (item.shape[0] // 2), item.shape[0] // 2, 0)

    def columns_of(whole):
        return lax.dynamic_slice_in_dim(whole, place * width, width, 1)

    packed = jnp.concatenate(
        [
            norm1_gain[0], norm1_bias[0], out_bias[0], norm2_gain[0], norm2_bias[0], down_bias[0],
            up_bias[0], qv_bias[0].reshape(-1),
        ]
    )
    length = packed.shape[0]
    packed = jnp.pad(packed.astype(f32), (0, -length % 1024)).reshape(-1, 128)

    def vectors_of(layer):
        own = small[layer]
        vectors = [own[:, :, i * part : (i + 1) * part].reshape(1, full) for i in range(6)]
        local = lax.dynamic_slice_in_dim(own, place, 1, 0)[0]
        b_up = local[:, 6 * part : 6 * part + part_up].reshape(-1)
        b_qv = local[:, 6 * part + part_up :].reshape(quads, heads, part_qv)
        b_qv = jnp.transpose(b_qv, (1, 0, 2)).reshape(heads, 2 * size)
        return (vectors, b_up, b_qv)

    def block(*rows):
        return jnp.concatenate(
            list(rows) + [jnp.zeros((8 - len(rows), full), f32)], axis=0
        )

    shards = (
        (qkv_weight[0].reshape(-1, heads * wide), 0),
        (out_weight[0].reshape(heads * size, -1), 1),
        (up_weight[0], 0),
        (down_weight[0], 1),
    )
    mask = allowed_mask(mine(segments))

    def whole_of(index, item):
        if index is None:
            return lax.all_gather(mine(item), "tensor", axis=1, tiled=True)
        return got[index]

    start = Group(0)
    at_v = gather_all(start, packed)
    at_x = gather_line(start, mine(tokens))
    at_w = [gather_plane(start, 0, item, axis, 100 + i) for i, (item, axis) in enumerate(shards)]
    at_c = gather_line(start, mine(cotangent))
    got = start.run()
    small = jnp.transpose(got[at_v].reshape(2, quads, tensors, -1)[..., :length], (0, 2, 1, 3))
    whole0, cot = whole_of(at_x, tokens), whole_of(at_c, cotangent)
    weights0 = [got[i] for i in at_w]
    vec0, b_up0, b_qv0 = vectors_of(0)
    vec1, b_up1, b_qv1 = vectors_of(1)

    def branch(call, source, weights, b_up, kept, vectors, flip):
        up, down = name_of(call, weights[2]), name_of(call, weights[3])
        shape = (whole0.shape[0], weights[2].shape[1])
        upper = call.result(shape, f32, pltpu.VMEM)
        active = call.result(shape, bf16, pltpu.VMEM)
        out_part = call.room(whole0.shape, bf16)
        produce = feed_forward(
            source, kept, vectors, up, down, name_of(call, b_up.reshape(1, -1)), upper, active,
            out_part,
        )
        made = chain_sum(
            call, "f2", out_part, None, flip=flip, start=tensors - 1, produce=produce
        )
        return made[0], upper, active, up, down

    def branch_back(call, source, up, down, upper, vectors, kept, flip, start):
        shape = (whole0.shape[0], units)
        grad_upper = call.result(shape, bf16, pltpu.VMEM)
        back_part = call.room(whole0.shape, bf16)
        produce = feed_back(source, up, down, upper, grad_upper, back_part)
        made = chain_sum(
            call, "b1", back_part, vectors, flip=flip, start=start, produce=produce, wide=source,
            kept=kept,
        )
        return made + (grad_upper,)

    def branch_grads(normed2, active, upstream, grad_upper):
        return (
            dot(normed2, grad_upper, ((0,), (0,))).astype(bf16),
            dot(active, upstream, ((0,), (0,))).astype(bf16),
            jnp.sum(grad_upper.astype(f32), axis=0),
        )

    units = hidden_units
    hop = tensors - 1

    partial, kept_a0 = attend(whole0, mask, vec0[0], vec0[1], weights0[0], b_qv0, weights0[1], heads)
    call = Group(1)
    at_v = call.operand(block(vec0[2], vec0[3], vec0[4], vec0[3], vec0[0], vec0[5]), pltpu.VMEM)
    a = chain_sum(call, "f1", partial, at_v, flip=True, wide=whole0)
    b = branch(call, a[0], weights0, b_up0, a[1], at_v, False)
    at_w2 = [gather_plane(call, 1, *shards[i], when=hop + 2) for i in (0, 1, 2, 3)]
    got = call.run()
    normed2_0, hidden0, whole1, upper0, active0 = (got[i[1]] for i in (a[0], a[1]) + b[:3])
    weights1 = [got[i] for i in at_w2]

    partial, kept_a1 = attend(
        whole1, mask, vec1[0], vec1[1], weights1[0], b_qv1, weights1[1], heads
    )
    call = Group(2)
    at_v = call.operand(block(vec1[2], vec1[3], vec1[4], vec1[3], vec1[0], vec1[5]), pltpu.VMEM)
    a = chain_sum(call, "f1", partial, at_v, wide=whole1)
    b = branch(call, a[0], weights1, b_up1, a[1], at_v, True)
    at_cot = call.operand(cot, pltpu.VMEM)
    c = branch_back(
        call, at_cot, b[3], b[4], b[1], call.operand(block(vec1[3]), pltpu.VMEM), a[1], False,
        2 * hop,
    )
    got = call.run()
    normed2_1, whole2, active1 = (got[i[1]] for i in (a[0], b[0], b[2]))
    ga, dhidden, sums_b1, grad_upper1 = (got[i[1]] for i in c)
    g_up1, g_down1, s_up1 = branch_grads(normed2_1, active1, cot, grad_upper1)

    partial, g_out1, g_qkv1, s_qv1 = attend_back(ga, kept_a1, weights1[0], weights1[1])
    call = Group(3)
    a = chain_sum(call, "b2", partial, block(vec1[0]), wide=whole1, kept=dhidden)
    c = branch_back(
        call, a[0], name_of(call, weights0[2]), name_of(call, weights0[3]), name_of(call, upper0),
        call.operand(block(vec0[3]), pltpu.VMEM), name_of(call, hidden0), True, hop,
    )
    at_g = [
        reduce_plane(call, 1, item, axis, (first_at, 2 * hop + 3))
        for item, axis, first_at in ((g_up1, 0, 1), (g_down1, 1, 2), (g_qkv1, 0, 3), (g_out1, 1, 3))
    ]
    got = call.run()
    grad1, sums_b2 = got[a[0][1]], got[a[2][1]]
    ga, dhidden, sums_a1, grad_upper0 = (got[i[1]] for i in c)
    r_up1, r_down1, r_qkv1, r_out1 = (got[i] for i in at_g)
    g_up0, g_down0, s_up0 = branch_grads(normed2_0, active0, grad1, grad_upper0)

    partial, g_out0, g_qkv0, s_qv0 = attend_back(ga, kept_a0, weights0[0], weights0[1])
    call = Group(4)
    a = chain_sum(call, "b2", partial, block(vec0[0]), flip=True, wide=whole0, kept=dhidden)
    at_g = [
        reduce_plane(call, 0, item, axis, (first_at, 1000))
        for item, axis, first_at in ((g_up0, 0, 1), (g_down0, 1, 2), (g_qkv0, 0, 3), (g_out0, 1, 3))
    ]
    got = call.run()
    grad0, sums_a2 = got[a[0][1]], got[a[2][1]]
    r_up0, r_down0, r_qkv0, r_out0 = (got[i] for i in at_g)

    def rows_of(sums_one, sums_two, up, qv):
        one = jnp.sum(sums_one.reshape(4, 8, full), axis=1)
        two = jnp.sum(sums_two.reshape(2, 8, full), axis=1)
        flat = [
            jnp.pad(item.reshape(1, -1), ((0, 0), (0, full - item.size))) for item in (up, qv)
        ]
        return jnp.concatenate(
            [two[0:1], two[1:2], one[2:3], one[0:1], one[1:2], one[3:4]] + flat, axis=0
        )

    call = Group(9)
    a = sum_vectors(
        call, jnp.stack([rows_of(sums_a1, sums_a2, s_up0, s_qv0), rows_of(sums_b1, sums_b2, s_up1, s_qv1)]), 6
    )
    vectors = call.run()[a]
    spot = (place * quads + quad) * part
    small_grads = [lax.dynamic_slice(vectors, (i, spot), (1, part))[0] for i in range(6)]
    g_up = lax.dynamic_slice(vectors, (6, quad * part_up), (1, part_up))[0]
    g_qv = vectors[7, : heads * 2 * size].reshape(heads, quads, part_qv)
    g_qv = lax.dynamic_slice_in_dim(g_qv, quad, 1, 1)[:, 0]

    def settle(of0, of1):
        of0, of1 = columns_of(of0), columns_of(of1)
        own = jnp.where(first, of0, of1)
        other = swap(jnp.where(first, of1, of0))
        return jnp.where(
            first, jnp.concatenate([own, other]), jnp.concatenate([other, own])
        )

    outputs = settle(whole1, whole2)
    input_grads = settle(grad0, grad1)
    totals = [
        jnp.where(first, one, two)
        for one, two in ((r_qkv0, r_qkv1), (r_out0, r_out1), (r_up0, r_up1), (r_down0, r_down1))
    ]
    result = (
        outputs,
        input_grads,
        small_grads[0],
        small_grads[1],
        totals[0].reshape(-1, heads, wide),
        g_qv,
        totals[1].reshape(heads, size, -1),
        small_grads[2],
        small_grads[3],
        small_grads[4],
        totals[2],
        g_up,
        totals[3],
        small_grads[5],
    )
    return tuple(item[None] for item in result)


def solution(mesh):
    vector = P("section", ("tensor", "seq"))
    return jax.shard_map(
        body,
        mesh=mesh,
        in_specs=(
            P("seq", "tensor"),
            P("seq", None),
            P("seq", "tensor"),
            vector,
            vector,
            P("section", "seq", "tensor", None),
            P("section", "tensor", "seq"),
            P("section", "tensor", None, "seq"),
            vector,
            vector,
            vector,
            P("section", "seq", "tensor"),
            vector,
            P("section", "tensor", "seq"),
            vector,
        ),
        out_specs=(
            P("section", "seq", "tensor"),
            P("section", "seq", "tensor"),
            vector,
            vector,
            P("section", "seq", "tensor", None),
            P("section", "tensor", "seq"),
            P("section", "tensor", None, "seq"),
            vector,
            vector,
            vector,
            P("section", "seq", "tensor"),
            vector,
            P("section", "tensor", "seq"),
            vector,
        ),
        check_vma=False,
    )
```

```python
import math

import jax
import jax.numpy as jnp
from jax import lax
from jax.experimental import pallas as pl
from jax.experimental.pallas import tpu as pltpu
from jax.sharding import PartitionSpec as P

epsilon = 1e-05
floor_value = -1e30
f32 = jnp.float32
bf16 = jnp.bfloat16
MESH = pl.DeviceIdType.MESH
CHUNKS = 4
HOP = 1
STEP = 16
TILE = 512
root = math.sqrt(2.0 / math.pi)
cubic = 0.044715


class Group:
    def __init__(self, number):
        self.number = number
        self.ins, self.in_specs = [], []
        self.outs, self.out_specs = [], []
        self.scratch = []
        self.count = 0
        self.jobs = []
        self.peers = set()
        self.ticks = 0
        self.rows = 0

    def operand(self, value, space):
        self.ins.append(value)
        self.in_specs.append(pl.BlockSpec(memory_space=space))
        return ("in", len(self.ins) - 1)

    def result(self, shape, dtype, space):
        self.outs.append(jax.ShapeDtypeStruct(shape, dtype))
        self.out_specs.append(pl.BlockSpec(memory_space=space))
        return ("out", len(self.outs) - 1)

    def room(self, shape, dtype):
        self.scratch.append(pltpu.VMEM(shape, dtype))
        return ("tmp", len(self.scratch) - 1)

    def scratch_shape(self, name):
        return self.scratch[name[1]].shape

    def sems(self, count):
        first = self.count
        self.count += count
        return first

    def run(self):
        n_in, n_out, n_tmp = len(self.ins), len(self.outs), len(self.scratch)

        def kernel(*refs):
            banks = {
                "in": refs[:n_in],
                "out": refs[n_in : n_in + n_out],
                "tmp": refs[n_in + n_out : n_in + n_out + n_tmp],
            }
            env = Env(banks, refs[-2], refs[-1])
            env.rows = self.rows
            env.greet(self.peers)
            stages = []
            for job in self.jobs:
                stages.extend(job(env))
            stages.sort(key=lambda item: item[0])
            for when, stage in stages:
                if when < 0:
                    stage()
            timed = [item for item in stages if 0 <= item[0] < self.ticks]

            def one(tick, carry):
                for tick_of in env.looped:
                    tick_of(tick)
                for when, stage in timed:
                    pl.when(tick == when)(stage)
                return carry

            if self.ticks:
                lax.fori_loop(0, self.ticks, one, 0)
            for when, stage in stages:
                if when >= self.ticks:
                    stage()
            env.finish()

        return pl.pallas_call(
            kernel,
            out_shape=tuple(self.outs),
            in_specs=self.in_specs,
            out_specs=tuple(self.out_specs),
            cost_estimate=pl.CostEstimate(
                flops=40_000_000_000, bytes_accessed=120_000_000, transcendentals=0
            ),
            scratch_shapes=self.scratch
            + [pltpu.SemaphoreType.DMA((self.count,)), pltpu.SemaphoreType.DMA((self.count,))],
            compiler_params=pltpu.CompilerParams(
                collective_id=self.number, has_side_effects=True, vmem_limit_bytes=48 << 20
            ),
        )(*self.ins)


class Env:
    def __init__(self, banks, send, recv):
        self.banks, self.send, self.recv = banks, send, recv
        self.core = lax.axis_index("section")
        self.quad = lax.axis_index("seq")
        self.place = lax.axis_index("tensor")
        self.cores = lax.axis_size("section")
        self.quads = lax.axis_size("seq")
        self.places = lax.axis_size("tensor")
        self.pending = []
        self.looped = []
        self.peers = [[self.reach(j, flip) for flip in (0, 1)] for j in range(self.quads)]
        self.line = [{"tensor": lax.rem(self.place + j, self.places)} for j in range(self.places)]
        self.other = 1 - self.core

    def __call__(self, name):
        return self.banks[name[0]][name[1]]

    def greet(self, peers):
        barrier = pltpu.get_barrier_semaphore()
        total = 0
        if "plane" in peers:
            for core in range(2):
                for j in range(self.quads):
                    if core == 0 and j == 0:
                        continue
                    pl.semaphore_signal(
                        barrier, inc=1, device_id=self.peer(j, core), device_id_type=MESH
                    )
                    total += 1
        if "line" in peers:
            for j in range(1, self.places):
                pl.semaphore_signal(barrier, inc=1, device_id=self.along(j), device_id_type=MESH)
                total += 1
        elif "next" in peers:
            for shift in (-1, 1):
                there = self.place + shift

                @pl.when((there >= 0) & (there < self.places))
                def _():
                    pl.semaphore_signal(
                        barrier, inc=1, device_id={"tensor": there}, device_id_type=MESH
                    )

            edge = (self.place == 0) | (self.place == self.places - 1)
            amount = total

            @pl.when(edge)
            def _():
                pl.semaphore_wait(barrier, amount + 1)

            @pl.when(jnp.logical_not(edge))
            def _():
                pl.semaphore_wait(barrier, amount + 2)

            return
        pl.semaphore_wait(barrier, total)

    def peer(self, j, flip):
        return self.peers[j][flip]

    def along(self, j):
        return self.line[j]

    def reach(self, j, flip):
        target = {"seq": lax.rem(self.quad + j, self.quads)}
        target["section"] = (1 - self.core) if flip else self.core
        return target

    def copy(self, source, target, sem, device):
        return pltpu.make_async_remote_copy(
            src_ref=source,
            dst_ref=target,
            send_sem=self.send.at[sem],
            recv_sem=self.recv.at[sem],
            device_id=device,
            device_id_type=MESH,
        )

    def start(self, source, target, sem, device, when=None):
        made = self.copy(source, target, sem, device)
        if when is None:
            made.start()
        else:
            pl.when(when)(made.start)
        self.pending.append((lambda: self.copy(source, target, sem, device).wait_send(), when))

    def arrived(self, target, sem):
        self.copy(target, target, sem, {"section": 1 - self.core}).wait_recv()

    def local(self, source, target, sem, when=None):
        made = pltpu.make_async_copy(source, target, self.send.at[sem])
        if when is None:
            made.start()
        else:
            pl.when(when)(made.start)
        self.pending.append(
            (lambda: pltpu.make_async_copy(source, target, self.send.at[sem]).wait(), when)
        )

    def finish(self):
        for wait, when in self.pending:
            if when is None:
                wait()
            else:
                pl.when(when)(wait)


def rows_loop(count, step, work):
    def one(i, carry):
        work(pl.multiple_of(i * step, step))
        return carry

    lax.fori_loop(0, count // step, one, 0)


def statistics(rows):
    average = jnp.mean(rows, axis=1, keepdims=True)
    variance = jnp.mean(rows * rows, axis=1, keepdims=True) - average * average
    scale = lax.rsqrt(variance + epsilon)
    return ((rows - average) * scale, scale)


def norm_backward(grad, centred, scale, gain):
    scaled = grad * gain
    total = jnp.mean(scaled, axis=1, keepdims=True)
    along = jnp.mean(scaled * centred, axis=1, keepdims=True)
    return scale * (scaled - total - centred * along)


def name_of(group, value):
    return value if isinstance(value, tuple) else group.operand(value, pltpu.VMEM)


def chain_sum(group, kind, part, vectors, flip=False, start=0, produce=None, wide=None, kept=None):
    if produce is None:
        count, width = part.shape
    else:
        count, width = group.scratch_shape(part)
    half = count // 2
    chunk = half // CHUNKS
    group.peers.add("next")
    n_part = name_of(group, part)
    n_vec = name_of(group, vectors) if vectors is not None else None
    n_wide = name_of(group, wide) if wide is not None else None
    n_half = name_of(group, kept) if kept is not None else None
    n_out = group.result((count, width), bf16, pltpu.VMEM)
    n_keep = group.result((half, width), f32, pltpu.VMEM) if kind in ("f1", "b1") else None
    sums = {"f1": 0, "f2": 0, "b1": 4, "b2": 2}[kind]
    n_sums = group.result((sums * 8, width), f32, pltpu.VMEM) if sums else None
    n_land = group.room((2, half, width), bf16)
    n_go = group.room((2, half, width), bf16)
    base = group.sems(4 * CHUNKS)
    last = lax.axis_size("tensor") - 1
    group.ticks = max(group.ticks, start + CHUNKS + 2 * HOP * last)

    def job(env):
        part, out, land, go = env(n_part), env(n_out), env(n_land), env(n_go)
        vec = env(n_vec) if n_vec else None
        wide = env(n_wide) if n_wide else None
        kept = env(n_half) if n_half else None
        keep = env(n_keep) if n_keep else None
        acc = env(n_sums) if n_sums else None

        def prepare():
            if acc is not None:
                acc[...] = jnp.zeros_like(acc)
            if keep is not None:
                keep[...] = jnp.zeros_like(keep)

        def add(row, value):
            acc[row * 8 : row * 8 + 8, :] += jnp.sum(
                value.reshape(STEP // 8, 8, width), axis=0
            )

        def close(side, k):
            def work(i):
                own = pl.ds(pl.multiple_of(k * chunk + i, STEP), STEP)
                at = pl.ds(pl.multiple_of(side * half + k * chunk + i, STEP), STEP)
                total = land[side, own, :].astype(f32) + part[at, :].astype(f32)
                if kind == "f1":
                    hidden = wide[at, :].astype(f32) + (total + vec[0:1, :])
                    keep[own, :] = hidden
                    centred, _ = statistics(hidden)
                    out[at, :] = (centred * vec[1:2, :] + vec[2:3, :]).astype(bf16)
                elif kind == "f2":
                    out[at, :] = total.astype(bf16)
                elif kind == "b1":
                    centred, scale = statistics(kept[own, :])
                    upstream = wide[at, :].astype(f32)
                    grad = upstream + norm_backward(total, centred, scale, vec[0:1, :])
                    keep[own, :] = grad
                    low = grad.astype(bf16)
                    out[at, :] = low
                    add(0, total * centred)
                    add(1, total)
                    add(2, low.astype(f32))
                    add(3, upstream)
                else:
                    centred, scale = statistics(wide[at, :].astype(f32))
                    grad = kept[own, :] + norm_backward(total, centred, scale, vec[0:1, :])
                    out[at, :] = grad.astype(bf16)
                    add(0, total * centred)
                    add(1, total)

            rows_loop(chunk, STEP, work)

        def layout(side):
            right = (side == 0) != flip
            steps = env.place if right else last - env.place
            there = env.place + 1 if right else env.place - 1
            back = env.place - 1 if right else env.place + 1
            return (
                steps, {"tensor": there}, {"tensor": back},
                base + 2 * side * CHUNKS, base + (2 * side + 1) * CHUNKS,
            )

        def slices(side, k):
            at = pl.ds(pl.multiple_of(side * half + k * chunk, STEP), chunk)
            own = pl.ds(pl.multiple_of(k * chunk, STEP), chunk)
            return at, own

        def due(k):
            return (k >= 0) & (k < CHUNKS)

        def forward(tick, side):
            steps, there, back, sem, sem_back = layout(side)
            k = tick - start - HOP * steps

            @pl.when(due(k))
            def _():
                at, own = slices(side, k)
                if produce is not None:
                    produce(env, side, k, at, own, steps == 0)

                @pl.when(steps > 0)
                def _():
                    env.arrived(land.at[side, own, :], sem + k)

                @pl.when(steps == last)
                def _():
                    close(side, k)
                    env.copy(out.at[at, :], out.at[at, :], sem_back + k, back).start()

                @pl.when(steps == 0)
                def _():
                    env.copy(part.at[at, :], land.at[side, own, :], sem + k, there).start()

                @pl.when((steps > 0) & (steps < last))
                def _():
                    def work(i):
                        i_own = pl.ds(pl.multiple_of(k * chunk + i, STEP), STEP)
                        i_at = pl.ds(pl.multiple_of(side * half + k * chunk + i, STEP), STEP)
                        go[side, i_own, :] = (
                            land[side, i_own, :].astype(f32) + part[i_at, :].astype(f32)
                        ).astype(bf16)

                    rows_loop(chunk, STEP, work)
                    env.copy(go.at[side, own, :], land.at[side, own, :], sem + k, there).start()

        def backward(tick, side):
            steps, there, back, sem, sem_back = layout(side)
            k = tick - start - HOP * (2 * last - steps)

            @pl.when(due(k) & (steps < last))
            def _():
                at, own = slices(side, k)
                env.arrived(out.at[at, :], sem_back + k)

                @pl.when(steps > 0)
                def _():
                    env.copy(out.at[at, :], out.at[at, :], sem_back + k, back).start()

        def tick_of(tick):
            for side in (0, 1):
                forward(tick, side)
            for side in (0, 1):
                backward(tick, side)

        def drain():
            for side in (0, 1):
                steps, there, back, sem, sem_back = layout(side)

                def one(k, carry, side=side, steps=steps, sem=sem, sem_back=sem_back):
                    at, own = slices(side, k)
                    piece = out.at[at, :]
                    near = {"section": 1 - env.core}

                    @pl.when(steps < last)
                    def _():
                        env.copy(piece, piece, sem + k, near).wait_send()

                    @pl.when(steps > 0)
                    def _():
                        env.copy(piece, piece, sem_back + k, near).wait_send()

                    return carry

                lax.fori_loop(0, CHUNKS, one, 0)

        env.looped.append(tick_of)
        return [(-30, prepare), (2000, drain)]

    group.jobs.append(job)
    return n_out, n_keep, n_sums


def column_loop(count, tile, work):
    def one(j, carry):
        work(pl.ds(pl.multiple_of(j * tile, tile), tile))
        return carry

    lax.fori_loop(0, count // tile, one, 0)


def stream(group, produce, start, flip, chunks):
    last = lax.axis_size("tensor") - 1
    group.ticks = max(group.ticks, start + chunks + HOP * last)

    def job(env):
        count = env.rows

        def tick_of(tick):
            for side in (0, 1):
                right = (side == 0) != flip
                steps = env.place if right else last - env.place
                k = tick - start - HOP * steps

                @pl.when((k >= 0) & (k < chunks))
                def _():
                    half = count // 2
                    chunk = half // chunks
                    at = pl.ds(pl.multiple_of(side * half + k * chunk, STEP), chunk)
                    own = pl.ds(pl.multiple_of(k * chunk, STEP), chunk)
                    produce(env, side, k, at, own, steps == 0)

        env.looped.append(tick_of)
        return []

    group.jobs.append(job)


def feed_forward(source, kept, vectors, up, down, b_up, upper, active, part):
    def produce(env, side, k, at, own, first):
        rows, residual, vec, w_up, w_down = (
            env(source), env(kept), env(vectors), env(up), env(down),
        )
        bias, o_upper, o_active, o_part = env(b_up), env(upper), env(active), env(part)
        units, width = w_down.shape

        def widen(cols):
            value = dot(rows[at, :], w_up[:, cols], ((1,), (0,))) + bias[0:1, cols]
            o_upper[at, cols] = value
            bent = jnp.tanh(root * (value + cubic * (value * value * value)))
            o_active[at, cols] = (0.5 * value * (1.0 + bent)).astype(bf16)

        def narrow(cols):
            value = dot(o_active[at, :], w_down[:, cols], ((1,), (0,)))
            extra = jnp.where(first, residual[own, cols] + vec[5:6, cols], 0.0)
            o_part[at, cols] = (value + extra).astype(bf16)

        column_loop(units, min(TILE, units), widen)
        column_loop(width, TILE, narrow)

    return produce


def feed_back(source, up, down, upper, grad_upper, part):
    def produce(env, side, k, at, own, first):
        rows, w_up, w_down = env(source), env(up), env(down)
        i_upper, o_grad, o_part = env(upper), env(grad_upper), env(part)
        units, width = w_down.shape

        def widen(cols):
            value = i_upper[at, cols]
            square = value * value
            bent = jnp.tanh(root * (value + cubic * (value * square)))
            slope = 0.5 * (1.0 + bent) + 0.5 * value * (1.0 - bent * bent) * (
                root * (1.0 + 3.0 * cubic * square)
            )
            grad = dot(rows[at, :], w_down[cols, :], ((1,), (1,)))
            o_grad[at, cols] = (grad * slope).astype(bf16)

        def narrow(cols):
            value = dot(o_grad[at, :], w_up[cols, :], ((1,), (1,)))
            o_part[at, cols] = value.astype(bf16)

        column_loop(units, min(TILE, units), widen)
        column_loop(width, TILE, narrow)

    return produce


def gather_line(group, piece):
    count, width = piece.shape
    places = lax.axis_size("tensor")
    if width % 128:
        return None
    group.peers.add("line")
    n_in = group.operand(piece, pltpu.VMEM)
    n_out = group.result((count, width * places), piece.dtype, pltpu.VMEM)
    base = group.sems(places)

    def job(env):
        source, out = env(n_in), env(n_out)

        def columns(index):
            return out.at[:, pl.ds(pl.multiple_of(index * width, width), width)]

        def begin():
            for j in sorted(range(1, places), key=lambda j: -min(j, places - j)):
                env.start(source, columns(env.place), base + j, env.along(j))
            env.local(source, columns(env.place), base)

        def end():
            for j in range(1, places):
                env.arrived(columns(lax.rem(env.place - j + places, places)), base + j)

        return [(-10, begin), (900, end)]

    group.jobs.append(job)
    return n_out[1]


def gather_all(group, piece):
    rows, width = piece.shape
    quads, places = lax.axis_size("seq"), lax.axis_size("tensor")
    group.peers.update(("plane", "line"))
    n_in = group.operand(piece, pltpu.VMEM)
    n_out = group.result((2, quads, places, rows, width), piece.dtype, pltpu.VMEM)
    base = group.sems(quads + places + 1)

    def job(env):
        source, out = env(n_in), env(n_out)
        mine = out.at[env.core, env.quad, env.place]

        def begin():
            mine[...] = source[...]
            for j in range(1, places):
                env.start(mine, mine, base + j, env.along(j))

        def second():
            for j in range(1, places):
                there = lax.rem(env.place - j + places, places)
                env.arrived(out.at[env.core, env.quad, there], base + j)
            line = out.at[env.core, env.quad]
            for j in range(1, quads):
                env.start(line, line, base + places + j, env.peer(j, 0))

        def third():
            for j in range(1, quads):
                there = lax.rem(env.quad - j + quads, quads)
                env.arrived(out.at[env.core, there], base + places + j)
            env.start(out.at[env.core], out.at[env.core], base, env.peer(0, 1))

        def end():
            env.arrived(out.at[1 - env.core], base)

        return [(-20, begin), (90, second), (91, third), (903, end)]

    group.jobs.append(job)
    return n_out[1]


def piece_of(ref, axis, slot, first, rows, shard, width):
    if axis == 0:
        return ref.at[pl.ds(pl.multiple_of(slot * shard + first, 16), rows), :]
    if not isinstance(first, int):
        first = pl.multiple_of(first, 16)
    return ref.at[
        pl.ds(first, rows), pl.ds(pl.multiple_of(slot * width, width), width)
    ]


def gather_plane(group, layer, shard, axis, when, inject_at=-4):
    rows, width = shard.shape
    half = rows // 2
    quads = lax.axis_size("seq")
    group.peers.add("plane")
    full = (rows * quads, width) if axis == 0 else (rows, width * quads)
    n_in = group.operand(shard, pl.ANY)
    n_out = group.result(full, shard.dtype, pl.ANY)
    base = group.sems(3 * quads + 1)

    def job(env):
        source, out = env(n_in), env(n_out)
        holder = env.core == layer

        def part(slot, core):
            return piece_of(out, axis, slot, core * half, half, rows, width)

        def whole(slot):
            return piece_of(out, axis, slot, 0, rows, rows, width)

        other = jnp.logical_not(holder)
        slots = [lax.rem(env.quad - j + quads, quads) for j in range(quads)]
        mine = [part(slot, env.core) for slot in slots]
        theirs = [part(slot, env.other) for slot in slots]
        own_slot = whole(env.quad)
        halves = [source.at[pl.ds(core * half, half), :] for core in (0, 1)]
        placed = [part(env.quad, core) for core in (0, 1)]

        placed_here = part(env.quad, env.core)
        order = (2, 1, 3) if quads == 4 else range(1, quads)

        def begin():
            env.start(source, own_slot, base + quads, env.peer(0, 1), holder)
            env.local(source, own_slot, base, holder)
            for j in order:
                env.start(halves[layer], placed[layer], base + j, env.peer(j, 0), holder)

        def inject():
            pl.when(other)(lambda: env.arrived(own_slot, base + quads))
            for j in order:
                env.start(placed_here, placed_here, base + j, env.peer(j, 0), other)

        def pass_on():
            for j in range(1, quads):
                env.arrived(mine[j], base + j)
                env.start(mine[j], mine[j], base + 2 * quads + j, env.peer(0, 1))

        def end():
            for j in range(1, quads):
                env.arrived(theirs[j], base + 2 * quads + j)

        return [(-5, begin), (inject_at, inject), (when, pass_on), (901, end)]

    group.jobs.append(job)
    return n_out[1]


def reduce_plane(group, layer, grad, axis, times):
    quads = lax.axis_size("seq")
    rows = grad.shape[0] // quads if axis == 0 else grad.shape[0]
    width = grad.shape[1] if axis == 0 else grad.shape[1] // quads
    half = rows // 2
    step = 32
    group.peers.add("plane")
    n_in = group.operand(grad, pltpu.VMEM)
    n_out = group.result((rows, width), f32, pltpu.VMEM)
    n_land = group.room((quads, half, width), bf16)
    n_sum = group.room((quads, half, width), bf16)
    n_far = group.room((quads, half, width), bf16)
    n_fin = group.room((half, width), f32)
    base = group.sems(2 * quads + 1)

    def job(env):
        mine, out, land, total, far, fin = (
            env(n_in), env(n_out), env(n_land), env(n_sum), env(n_far), env(n_fin),
        )
        holder = env.core == layer
        other = jnp.logical_not(holder)
        order = [2, 1, 3, 0] if quads == 4 else list(range(1, quads)) + [0]
        slots = [lax.rem(env.quad + j, quads) for j in range(quads)]
        mine_of = [
            piece_of(mine, axis, slot, env.core * half, half, rows, width) for slot in slots
        ]
        their_of = [
            piece_of(mine, axis, slot, env.other * half, half, rows, width) for slot in slots
        ]
        lands = [land.at[slot] for slot in slots]
        totals = [total.at[slot] for slot in slots]
        fars = [far.at[j] for j in range(quads)]
        spot_mine = out.at[pl.ds(pl.multiple_of(env.core * half, 16), half), :]
        spot_other = out.at[pl.ds(pl.multiple_of(env.other * half, 16), half), :]

        def begin():
            for j in order:
                env.start(their_of[j], lands[j], base + j, env.peer(0, 1))

        def middle():
            for j in order:
                slot = slots[j]
                env.arrived(lands[j], base + j)
                own = mine_of[j]

                def work(i, slot=slot, own=own):
                    at = pl.ds(i, step)
                    total[slot, at, :] = (
                        own[at, :].astype(f32) + land[slot, at, :].astype(f32)
                    ).astype(bf16)

                rows_loop(half, step, work)
                if j:
                    env.start(totals[j], fars[j], base + quads + j, env.peer(j, 0))

        def close():
            for j in range(1, quads):
                env.arrived(far.at[j], base + quads + j)

            def work(i):
                at = pl.ds(i, step)
                value = total[env.quad, at, :].astype(f32)
                for j in range(1, quads):
                    value = value + far[j, at, :].astype(f32)
                fin[at, :] = value

            rows_loop(half, step, work)
            env.start(fin, spot_mine, base + 2 * quads, env.peer(0, 1), other)
            env.local(fin, spot_mine, base + quads, holder)

        def end():
            @pl.when(holder)
            def _():
                env.arrived(spot_other, base + 2 * quads)

        return [(times[2], begin), (times[0], middle), (times[1], close), (1500, end)]

    group.jobs.append(job)
    return n_out[1]


def sum_vectors(group, pair, shared, late):
    rows, width = pair.shape[1:]
    quads, places = lax.axis_size("seq"), lax.axis_size("tensor")
    group.peers.update(("plane", "line"))
    n_in = group.operand(pair, pltpu.VMEM)
    n_out = group.result((rows, width), f32, pltpu.VMEM)
    n_near = group.room((rows, width), f32)
    n_full = group.room((2, rows, width), f32)
    n_one = group.room((rows, width), f32)
    n_far = group.room((quads, rows, width), f32)
    n_two = group.room((rows, width), f32)
    n_end = group.room((places, rows, width), f32)
    base = group.sems(quads + places)

    def job(env):
        given, out, near, one, far, two, ends = (
            env(n_in), env(n_out), env(n_near), env(n_one), env(n_far), env(n_two), env(n_end),
        )
        mine = env(n_full)

        def go():
            mine[...] = given[...]
            for row in range(late[1]):
                extra = env(late[0])[row * 8 : row * 8 + 8, :]
                mine[0, row : row + 1, :] = jnp.sum(extra, axis=0, keepdims=True)
            env.start(mine.at[1 - env.core], near, base, env.peer(0, 1))
            env.arrived(near, base)
            one[...] = mine[env.core] + near[...]
            for j in range(1, quads):
                env.start(one, far.at[j], base + j, env.peer(j, 0))
            value = one[...]
            for j in range(1, quads):
                env.arrived(far.at[j], base + j)
                value = value + far[j]
            two[...] = value
            for j in range(1, places):
                env.start(two, ends.at[j], base + quads + j, env.along(j))
            for j in range(1, places):
                env.arrived(ends.at[j], base + quads + j)
                value = value + ends[j]
            row = lax.broadcasted_iota(jnp.int32, value.shape, 0)
            out[...] = jnp.where(row < shared, value, two[...])

        return [(890, go)]

    group.jobs.append(job)
    return n_out[1]


def allowed_mask(segment):
    length = segment.shape[1]
    place = lax.broadcasted_iota(jnp.int32, (length, length), 0)
    other = lax.broadcasted_iota(jnp.int32, (length, length), 1)
    same = segment[:, :, None] == segment[:, None, :]
    return (same & (other <= place)[None])[:, None]


def dot(left, right, dims):
    return lax.dot_general(left, right, (dims, ((), ())), preferred_element_type=f32)


def attend(whole, mask, gain, bias, w_qkv, b_qv, w_out, heads):
    count = whole.shape[0]
    size = w_qkv.shape[1] // heads // 3
    shape4 = (mask.shape[0], mask.shape[2], heads, size)
    factor = 1.0 / math.sqrt(size)
    normed = (statistics(whole.astype(f32))[0] * gain + bias).astype(bf16)
    mixed = dot(normed, w_qkv, ((1,), (0,))).reshape(count, heads, 3 * size)
    query = (mixed[..., :size] + b_qv[:, :size]).astype(bf16).reshape(shape4)
    keys = mixed[..., size : 2 * size].astype(bf16).reshape(shape4)
    values = (mixed[..., 2 * size :] + b_qv[:, size:]).astype(bf16).reshape(shape4)
    scores = jnp.einsum("sqhe,skhe->shqk", query, keys, preferred_element_type=f32) * factor
    masked = jnp.where(mask, scores, floor_value)
    raised = jnp.exp(masked - jnp.max(masked, axis=-1, keepdims=True))
    chance = raised / jnp.sum(raised, axis=-1, keepdims=True)
    low = chance.astype(bf16)
    context = jnp.einsum("shqk,skhe->sqhe", low, values, preferred_element_type=f32)
    context = context.reshape(count, heads * size).astype(bf16)
    partial = dot(context, w_out, ((1,), (0,))).astype(bf16)
    return (partial, (normed, query, keys, values, chance, low, context))


def attend_back(whole_ga, kept, w_qkv, w_out):
    normed, query, keys, values, chance, low, context = kept
    count = whole_ga.shape[0]
    heads, size = query.shape[2:]
    factor = 1.0 / math.sqrt(size)
    grad_context = dot(whole_ga, w_out, ((1,), (1,))).astype(bf16).reshape(query.shape)
    grad_chance = jnp.einsum("sqhe,skhe->shqk", grad_context, values, preferred_element_type=f32)
    delta = jnp.sum(grad_chance * chance, axis=-1, keepdims=True)
    grad_scores = (chance * (grad_chance - delta)).astype(bf16)
    grad_query = (
        jnp.einsum("shqk,skhe->sqhe", grad_scores, keys, preferred_element_type=f32) * factor
    ).astype(bf16)
    grad_keys = (
        jnp.einsum("shqk,sqhe->skhe", grad_scores, query, preferred_element_type=f32) * factor
    ).astype(bf16)
    grad_values = jnp.einsum(
        "shqk,sqhe->skhe", low, grad_context, preferred_element_type=f32
    ).astype(bf16)
    grad_mixed = jnp.concatenate([grad_query, grad_keys, grad_values], axis=-1).reshape(
        count, heads * 3 * size
    )
    partial = dot(grad_mixed, w_qkv, ((1,), (1,))).astype(bf16)
    grad_out_w = dot(context, whole_ga, ((0,), (0,))).astype(bf16)
    grad_qkv = dot(normed, grad_mixed, ((0,), (0,))).astype(bf16)
    grad_qv = jnp.concatenate(
        [
            jnp.sum(grad_query.astype(f32), axis=(0, 1)),
            jnp.sum(grad_values.astype(f32), axis=(0, 1)),
        ],
        axis=-1,
    )
    return (partial, grad_out_w, grad_qkv, grad_qv)


def swap(item):
    return lax.ppermute(item, "section", [(0, 1), (1, 0)])


def body(
    tokens, segments, cotangent, norm1_gain, norm1_bias, qkv_weight, qv_bias, out_weight, out_bias,
    norm2_gain, norm2_bias, up_weight, up_bias, down_weight, down_bias,
):
    section = lax.axis_index("section")
    place = lax.axis_index("tensor")
    quad = lax.axis_index("seq")
    tensors = lax.axis_size("tensor")
    quads = lax.axis_size("seq")
    first = section == 0
    rows_all, width = tokens.shape
    full = width * tensors
    heads, wide = qkv_weight.shape[2:]
    size = wide // 3
    part = norm1_gain.shape[1]
    part_up = up_bias.shape[1]
    part_qv = qv_bias.shape[2]
    hidden_units = up_weight.shape[2]

    def mine(item):
        return lax.dynamic_slice_in_dim(item, section * (item.shape[0] // 2), item.shape[0] // 2, 0)

    def columns_of(whole):
        return lax.dynamic_slice_in_dim(whole, place * width, width, 1)

    packed = jnp.concatenate(
        [
            norm1_gain[0], norm1_bias[0], out_bias[0], norm2_gain[0], norm2_bias[0], down_bias[0],
            up_bias[0], qv_bias[0].reshape(-1),
        ]
    )
    length = packed.shape[0]
    packed = jnp.pad(packed.astype(f32), (0, -length % 1024)).reshape(-1, 128)

    def vectors_of(layer):
        own = small[layer]
        vectors = [own[:, :, i * part : (i + 1) * part].reshape(1, full) for i in range(6)]
        local = lax.dynamic_slice_in_dim(own, place, 1, 0)[0]
        b_up = local[:, 6 * part : 6 * part + part_up].reshape(-1)
        b_qv = local[:, 6 * part + part_up :].reshape(quads, heads, part_qv)
        b_qv = jnp.transpose(b_qv, (1, 0, 2)).reshape(heads, 2 * size)
        return (vectors, b_up, b_qv)

    def block(*rows):
        return jnp.concatenate(
            list(rows) + [jnp.zeros((8 - len(rows), full), f32)], axis=0
        )

    shards = (
        (qkv_weight[0].reshape(-1, heads * wide), 0),
        (out_weight[0].reshape(heads * size, -1), 1),
        (up_weight[0], 0),
        (down_weight[0], 1),
    )
    mask = allowed_mask(mine(segments))

    def whole_of(index, item):
        if index is None:
            return lax.all_gather(mine(item), "tensor", axis=1, tiled=True)
        return got[index]

    start = Group(0)
    at_v = gather_all(start, packed)
    at_x = gather_line(start, mine(tokens))
    at_w = [gather_plane(start, 0, item, axis, 100 + i) for i, (item, axis) in enumerate(shards)]
    got = start.run()
    small = jnp.transpose(got[at_v].reshape(2, quads, tensors, -1)[..., :length], (0, 2, 1, 3))
    whole0 = whole_of(at_x, tokens)
    cot = lax.all_gather(mine(cotangent), "tensor", axis=1, tiled=True)
    weights0 = [got[i] for i in at_w]
    vec0, b_up0, b_qv0 = vectors_of(0)
    vec1, b_up1, b_qv1 = vectors_of(1)

    def branch(call, source, weights, b_up, kept, vectors, flip, chain=True):
        up, down = name_of(call, weights[2]), name_of(call, weights[3])
        shape = (whole0.shape[0], weights[2].shape[1])
        upper = call.result(shape, f32, pltpu.VMEM)
        active = call.result(shape, bf16, pltpu.VMEM)
        if chain:
            out_part = call.room(whole0.shape, bf16)
        else:
            out_part = call.result(whole0.shape, bf16, pltpu.VMEM)
        produce = feed_forward(
            source, kept, vectors, up, down, name_of(call, b_up.reshape(1, -1)), upper, active,
            out_part,
        )
        if not chain:
            call.rows = whole0.shape[0]
            stream(call, produce, hop, flip, CHUNKS)
            return out_part, upper, active, up, down
        made = chain_sum(call, "f2", out_part, None, flip=flip, start=hop, produce=produce)
        return made[0], upper, active, up, down

    def branch_back(call, source, up, down, upper, vectors, kept, flip, start):
        shape = (whole0.shape[0], units)
        grad_upper = call.result(shape, bf16, pltpu.VMEM)
        back_part = call.room(whole0.shape, bf16)
        produce = feed_back(source, up, down, upper, grad_upper, back_part)
        made = chain_sum(
            call, "b1", back_part, vectors, flip=flip, start=start, produce=produce, wide=source,
            kept=kept,
        )
        return made + (grad_upper,)

    def branch_grads(normed2, active, upstream, grad_upper):
        return (
            dot(normed2, grad_upper, ((0,), (0,))).astype(bf16),
            dot(active, upstream, ((0,), (0,))).astype(bf16),
            jnp.sum(grad_upper.astype(f32), axis=0),
        )

    units = hidden_units
    hop = HOP * (tensors - 1)

    partial, kept_a0 = attend(whole0, mask, vec0[0], vec0[1], weights0[0], b_qv0, weights0[1], heads)
    call = Group(1)
    at_v = call.operand(block(vec0[2], vec0[3], vec0[4], vec0[3], vec0[0], vec0[5]), pltpu.VMEM)
    a = chain_sum(call, "f1", partial, at_v, flip=True, wide=whole0)
    b = branch(call, a[0], weights0, b_up0, a[1], at_v, False)
    at_w2 = [
        gather_plane(call, 1, *shards[i], when=when, inject_at=2 * HOP)
        for i, when in zip(range(4), (hop + 1, hop + 2, 2 * hop + 1, 2 * hop + 2))
    ]
    got = call.run()
    normed2_0, hidden0, whole1, upper0, active0 = (got[i[1]] for i in (a[0], a[1]) + b[:3])
    weights1 = [got[i] for i in at_w2]

    partial, kept_a1 = attend(
        whole1, mask, vec1[0], vec1[1], weights1[0], b_qv1, weights1[1], heads
    )
    call = Group(2)
    at_v = call.operand(block(vec1[2], vec1[3], vec1[4], vec1[3], vec1[0], vec1[5]), pltpu.VMEM)
    a = chain_sum(call, "f1", partial, at_v, wide=whole1)
    b = branch(call, a[0], weights1, b_up1, a[1], at_v, True, chain=False)
    at_cot = call.operand(cot, pltpu.VMEM)
    c = branch_back(
        call, at_cot, b[3], b[4], b[1], call.operand(block(vec1[3]), pltpu.VMEM), a[1], False,
        2 * hop,
    )
    got = call.run()
    normed2_1, last_part, active1 = (got[i[1]] for i in (a[0], b[0], b[2]))
    columns2 = lax.psum_scatter(last_part, "tensor", scatter_dimension=1, tiled=True)
    ga, dhidden, sums_b1, grad_upper1 = (got[i[1]] for i in c)
    g_up1, g_down1, s_up1 = branch_grads(normed2_1, active1, cot, grad_upper1)

    partial, g_out1, g_qkv1, s_qv1 = attend_back(ga, kept_a1, weights1[0], weights1[1])
    call = Group(3)
    a = chain_sum(call, "b2", partial, block(vec1[0]), wide=whole1, kept=dhidden)
    c = branch_back(
        call, a[0], name_of(call, weights0[2]), name_of(call, weights0[3]), name_of(call, upper0),
        call.operand(block(vec0[3]), pltpu.VMEM), name_of(call, hidden0), True, hop,
    )
    at_g = [
        reduce_plane(call, 1, item, axis, (first_at, 2 * hop + 3, begin_at))
        for item, axis, first_at, begin_at in (
            (g_up1, 0, 1, -8), (g_down1, 1, 2, 1), (g_qkv1, 0, 3, 2), (g_out1, 1, 3, 2)
        )
    ]
    got = call.run()
    grad1, sums_b2 = got[a[0][1]], got[a[2][1]]
    ga, dhidden, sums_a1, grad_upper0 = (got[i[1]] for i in c)
    r_up1, r_down1, r_qkv1, r_out1 = (got[i] for i in at_g)
    g_up0, g_down0, s_up0 = branch_grads(normed2_0, active0, grad1, grad_upper0)

    partial, g_out0, g_qkv0, s_qv0 = attend_back(ga, kept_a0, weights0[0], weights0[1])
    def rows_of(sums_one, sums_two, up, qv):
        one = jnp.sum(sums_one.reshape(4, 8, full), axis=1)
        two = jnp.sum(sums_two.reshape(2, 8, full), axis=1)
        flat = [
            jnp.pad(item.reshape(1, -1), ((0, 0), (0, full - item.size))) for item in (up, qv)
        ]
        return jnp.concatenate([two, one[2:3], one[0:2], one[3:4]] + flat, axis=0)

    small_sums = jnp.stack(
        [
            rows_of(sums_a1, jnp.zeros((16, full), f32), s_up0, s_qv0),
            rows_of(sums_b1, sums_b2, s_up1, s_qv1),
        ]
    )
    call = Group(4)
    a = chain_sum(call, "b2", partial, block(vec0[0]), flip=True, wide=whole0, kept=dhidden)
    at_g = [
        reduce_plane(call, 0, item, axis, (first_at, 1000, begin_at))
        for item, axis, first_at, begin_at in (
            (g_up0, 0, 1, -8), (g_down0, 1, 3, 2), (g_qkv0, 0, 5, 4), (g_out0, 1, 5, 4)
        )
    ]
    at_v = sum_vectors(call, small_sums, 6, (a[2], 2))
    got = call.run()
    grad0, vectors = got[a[0][1]], got[at_v]
    r_up0, r_down0, r_qkv0, r_out0 = (got[i] for i in at_g)

    spot = (place * quads + quad) * part
    small_grads = [lax.dynamic_slice(vectors, (i, spot), (1, part))[0] for i in range(6)]
    g_up = lax.dynamic_slice(vectors, (6, quad * part_up), (1, part_up))[0]
    g_qv = vectors[7, : heads * 2 * size].reshape(heads, quads, part_qv)
    g_qv = lax.dynamic_slice_in_dim(g_qv, quad, 1, 1)[:, 0]

    def settle(of0, of1):
        own = jnp.where(first, of0, of1)
        other = swap(jnp.where(first, of1, of0))
        return jnp.where(
            first, jnp.concatenate([own, other]), jnp.concatenate([other, own])
        )

    outputs = settle(columns_of(whole1), columns2)
    input_grads = settle(columns_of(grad0), columns_of(grad1))
    totals = [
        jnp.where(first, one, two)
        for one, two in ((r_qkv0, r_qkv1), (r_out0, r_out1), (r_up0, r_up1), (r_down0, r_down1))
    ]
    result = (
        outputs,
        input_grads,
        small_grads[0],
        small_grads[1],
        totals[0].reshape(-1, heads, wide),
        g_qv,
        totals[1].reshape(heads, size, -1),
        small_grads[2],
        small_grads[3],
        small_grads[4],
        totals[2],
        g_up,
        totals[3],
        small_grads[5],
    )
    return tuple(item[None] for item in result)


def solution(mesh):
    vector = P("section", ("tensor", "seq"))
    return jax.shard_map(
        body,
        mesh=mesh,
        in_specs=(
            P("seq", "tensor"),
            P("seq", None),
            P("seq", "tensor"),
            vector,
            vector,
            P("section", "seq", "tensor", None),
            P("section", "tensor", "seq"),
            P("section", "tensor", None, "seq"),
            vector,
            vector,
            vector,
            P("section", "seq", "tensor"),
            vector,
            P("section", "tensor", "seq"),
            vector,
        ),
        out_specs=(
            P("section", "seq", "tensor"),
            P("section", "seq", "tensor"),
            vector,
            vector,
            P("section", "seq", "tensor", None),
            P("section", "tensor", "seq"),
            P("section", "tensor", None, "seq"),
            vector,
            vector,
            vector,
            P("section", "seq", "tensor"),
            vector,
            P("section", "tensor", "seq"),
            vector,
        ),
        check_vma=False,
    )
```

```python
import math

import jax
import jax.numpy as jnp
from jax import lax
from jax.experimental import pallas as pl
from jax.experimental.pallas import tpu as pltpu
from jax.sharding import PartitionSpec as P

epsilon = 1e-05
floor_value = -1e30
f32 = jnp.float32
bf16 = jnp.bfloat16
MESH = pl.DeviceIdType.MESH
CHUNKS = 4
HOP = 1
STEP = 16
TILE = 512
root = math.sqrt(2.0 / math.pi)
cubic = 0.044715


class Group:
    def __init__(self, number):
        self.number = number
        self.ins, self.in_specs = [], []
        self.outs, self.out_specs = [], []
        self.scratch = []
        self.count = 0
        self.jobs = []
        self.peers = set()
        self.ticks = 0
        self.rows = 0

    def operand(self, value, space):
        self.ins.append(value)
        self.in_specs.append(pl.BlockSpec(memory_space=space))
        return ("in", len(self.ins) - 1)

    def result(self, shape, dtype, space):
        self.outs.append(jax.ShapeDtypeStruct(shape, dtype))
        self.out_specs.append(pl.BlockSpec(memory_space=space))
        return ("out", len(self.outs) - 1)

    def room(self, shape, dtype):
        self.scratch.append(pltpu.VMEM(shape, dtype))
        return ("tmp", len(self.scratch) - 1)

    def scratch_shape(self, name):
        return self.scratch[name[1]].shape

    def sems(self, count):
        first = self.count
        self.count += count
        return first

    def run(self):
        n_in, n_out, n_tmp = len(self.ins), len(self.outs), len(self.scratch)

        def kernel(*refs):
            banks = {
                "in": refs[:n_in],
                "out": refs[n_in : n_in + n_out],
                "tmp": refs[n_in + n_out : n_in + n_out + n_tmp],
            }
            env = Env(banks, refs[-2], refs[-1])
            env.rows = self.rows
            env.greet(self.peers)
            stages = []
            for job in self.jobs:
                stages.extend(job(env))
            stages.sort(key=lambda item: item[0])
            for when, stage in stages:
                if when < 0:
                    stage()
            timed = [item for item in stages if 0 <= item[0] < self.ticks]

            def one(tick, carry):
                for tick_of in env.looped:
                    tick_of(tick)
                for when, stage in timed:
                    pl.when(tick == when)(stage)
                return carry

            if self.ticks:
                lax.fori_loop(0, self.ticks, one, 0)
            for when, stage in stages:
                if when >= self.ticks:
                    stage()
            env.finish()

        return pl.pallas_call(
            kernel,
            out_shape=tuple(self.outs),
            in_specs=self.in_specs,
            out_specs=tuple(self.out_specs),
            cost_estimate=pl.CostEstimate(
                flops=40_000_000_000, bytes_accessed=120_000_000, transcendentals=0
            ),
            scratch_shapes=self.scratch
            + [pltpu.SemaphoreType.DMA((self.count,)), pltpu.SemaphoreType.DMA((self.count,))],
            compiler_params=pltpu.CompilerParams(
                collective_id=self.number, has_side_effects=True, vmem_limit_bytes=48 << 20
            ),
        )(*self.ins)


class Env:
    def __init__(self, banks, send, recv):
        self.banks, self.send, self.recv = banks, send, recv
        self.core = lax.axis_index("section")
        self.quad = lax.axis_index("seq")
        self.place = lax.axis_index("tensor")
        self.cores = lax.axis_size("section")
        self.quads = lax.axis_size("seq")
        self.places = lax.axis_size("tensor")
        self.pending = []
        self.looped = []
        self.peers = [[self.reach(j, flip) for flip in (0, 1)] for j in range(self.quads)]
        self.line = [{"tensor": lax.rem(self.place + j, self.places)} for j in range(self.places)]
        self.other = 1 - self.core

    def __call__(self, name):
        return self.banks[name[0]][name[1]]

    def greet(self, peers):
        barrier = pltpu.get_barrier_semaphore()
        total = 0
        if "plane" in peers:
            for core in range(2):
                for j in range(self.quads):
                    if core == 0 and j == 0:
                        continue
                    pl.semaphore_signal(
                        barrier, inc=1, device_id=self.peer(j, core), device_id_type=MESH
                    )
                    total += 1
        if "line" in peers:
            for j in range(1, self.places):
                pl.semaphore_signal(barrier, inc=1, device_id=self.along(j), device_id_type=MESH)
                total += 1
        elif "next" in peers:
            for shift in (-1, 1):
                there = self.place + shift

                @pl.when((there >= 0) & (there < self.places))
                def _():
                    pl.semaphore_signal(
                        barrier, inc=1, device_id={"tensor": there}, device_id_type=MESH
                    )

            edge = (self.place == 0) | (self.place == self.places - 1)
            amount = total

            @pl.when(edge)
            def _():
                pl.semaphore_wait(barrier, amount + 1)

            @pl.when(jnp.logical_not(edge))
            def _():
                pl.semaphore_wait(barrier, amount + 2)

            return
        pl.semaphore_wait(barrier, total)

    def peer(self, j, flip):
        return self.peers[j][flip]

    def along(self, j):
        return self.line[j]

    def reach(self, j, flip):
        target = {"seq": lax.rem(self.quad + j, self.quads)}
        target["section"] = (1 - self.core) if flip else self.core
        return target

    def copy(self, source, target, sem, device):
        return pltpu.make_async_remote_copy(
            src_ref=source,
            dst_ref=target,
            send_sem=self.send.at[sem],
            recv_sem=self.recv.at[sem],
            device_id=device,
            device_id_type=MESH,
        )

    def start(self, source, target, sem, device, when=None):
        made = self.copy(source, target, sem, device)
        if when is None:
            made.start()
        else:
            pl.when(when)(made.start)
        self.pending.append((lambda: self.copy(source, target, sem, device).wait_send(), when))

    def arrived(self, target, sem):
        self.copy(target, target, sem, {"section": 1 - self.core}).wait_recv()

    def local(self, source, target, sem, when=None):
        made = pltpu.make_async_copy(source, target, self.send.at[sem])
        if when is None:
            made.start()
        else:
            pl.when(when)(made.start)
        self.pending.append(
            (lambda: pltpu.make_async_copy(source, target, self.send.at[sem]).wait(), when)
        )

    def finish(self):
        for wait, when in self.pending:
            if when is None:
                wait()
            else:
                pl.when(when)(wait)


def rows_loop(count, step, work):
    def one(i, carry):
        work(pl.multiple_of(i * step, step))
        return carry

    lax.fori_loop(0, count // step, one, 0)


def statistics(rows):
    average = jnp.mean(rows, axis=1, keepdims=True)
    variance = jnp.mean(rows * rows, axis=1, keepdims=True) - average * average
    scale = lax.rsqrt(variance + epsilon)
    return ((rows - average) * scale, scale)


def norm_backward(grad, centred, scale, gain):
    scaled = grad * gain
    total = jnp.mean(scaled, axis=1, keepdims=True)
    along = jnp.mean(scaled * centred, axis=1, keepdims=True)
    return scale * (scaled - total - centred * along)


def name_of(group, value):
    return value if isinstance(value, tuple) else group.operand(value, pltpu.VMEM)


def chain_sum(group, kind, part, vectors, flip=False, start=0, produce=None, wide=None, kept=None, spread=False):
    if produce is None:
        count, width = part.shape
    else:
        count, width = group.scratch_shape(part)
    half = count // 2
    chunk = half // CHUNKS
    group.peers.add("next")
    n_part = name_of(group, part)
    n_vec = name_of(group, vectors) if vectors is not None else None
    n_wide = name_of(group, wide) if wide is not None else None
    n_half = name_of(group, kept) if kept is not None else None
    n_out = group.result((count, width), bf16, pltpu.VMEM)
    n_keep = group.result((half, width), f32, pltpu.VMEM) if kind in ("f1", "b1") else None
    sums = {"f1": 0, "f2": 0, "b1": 4, "b2": 2}[kind]
    n_sums = group.result((sums * 8, width), f32, pltpu.VMEM) if sums else None
    n_land = group.room((2, half, width), bf16)
    n_go = group.room((2, half, width), bf16)
    base = group.sems(4 * CHUNKS)
    last = lax.axis_size("tensor") - 1
    places = last + 1
    piece = width // places
    spread = spread and piece % 128 == 0
    if spread:
        group.peers.add("line")
        base_far = group.sems(2 * places * CHUNKS)
    group.ticks = max(group.ticks, start + CHUNKS + (1 if spread else 2) * HOP * last)

    def job(env):
        part, out, land, go = env(n_part), env(n_out), env(n_land), env(n_go)
        vec = env(n_vec) if n_vec else None
        wide = env(n_wide) if n_wide else None
        kept = env(n_half) if n_half else None
        keep = env(n_keep) if n_keep else None
        acc = env(n_sums) if n_sums else None

        def prepare():
            if acc is not None:
                acc[...] = jnp.zeros_like(acc)
            if keep is not None:
                keep[...] = jnp.zeros_like(keep)

        def add(row, value):
            acc[row * 8 : row * 8 + 8, :] += jnp.sum(
                value.reshape(STEP // 8, 8, width), axis=0
            )

        def close(side, k):
            def work(i):
                own = pl.ds(pl.multiple_of(k * chunk + i, STEP), STEP)
                at = pl.ds(pl.multiple_of(side * half + k * chunk + i, STEP), STEP)
                total = land[side, own, :].astype(f32) + part[at, :].astype(f32)
                if kind == "f1":
                    hidden = wide[at, :].astype(f32) + (total + vec[0:1, :])
                    keep[own, :] = hidden
                    centred, _ = statistics(hidden)
                    out[at, :] = (centred * vec[1:2, :] + vec[2:3, :]).astype(bf16)
                elif kind == "f2":
                    out[at, :] = total.astype(bf16)
                elif kind == "b1":
                    centred, scale = statistics(kept[own, :])
                    upstream = wide[at, :].astype(f32)
                    grad = upstream + norm_backward(total, centred, scale, vec[0:1, :])
                    keep[own, :] = grad
                    low = grad.astype(bf16)
                    out[at, :] = low
                    add(0, total * centred)
                    add(1, total)
                    add(2, low.astype(f32))
                    add(3, upstream)
                else:
                    centred, scale = statistics(wide[at, :].astype(f32))
                    grad = kept[own, :] + norm_backward(total, centred, scale, vec[0:1, :])
                    out[at, :] = grad.astype(bf16)
                    add(0, total * centred)
                    add(1, total)

            rows_loop(chunk, STEP, work)

        def layout(side):
            right = (side == 0) != flip
            steps = env.place if right else last - env.place
            there = env.place + 1 if right else env.place - 1
            back = env.place - 1 if right else env.place + 1
            return (
                steps, {"tensor": there}, {"tensor": back},
                base + 2 * side * CHUNKS, base + (2 * side + 1) * CHUNKS,
            )

        def slices(side, k):
            at = pl.ds(pl.multiple_of(side * half + k * chunk, STEP), chunk)
            own = pl.ds(pl.multiple_of(k * chunk, STEP), chunk)
            return at, own

        def columns_at(at, index):
            return out.at[at, pl.ds(pl.multiple_of(index * piece, piece), piece)]

        def due(k):
            return (k >= 0) & (k < CHUNKS)

        def forward(tick, side):
            steps, there, back, sem, sem_back = layout(side)
            k = tick - start - HOP * steps

            @pl.when(due(k))
            def _():
                at, own = slices(side, k)
                if produce is not None:
                    produce(env, side, k, at, own, steps == 0)

                @pl.when(steps > 0)
                def _():
                    env.arrived(land.at[side, own, :], sem + k)

                @pl.when(steps == last)
                def _():
                    close(side, k)
                    if spread:
                        for j in range(1, places):
                            far_piece = columns_at(at, lax.rem(env.place + j, places))
                            env.copy(
                                far_piece, far_piece, base_far + (side * places + j) * CHUNKS + k,
                                env.along(j),
                            ).start()
                    else:
                        env.copy(out.at[at, :], out.at[at, :], sem_back + k, back).start()

                @pl.when(steps == 0)
                def _():
                    env.copy(part.at[at, :], land.at[side, own, :], sem + k, there).start()

                @pl.when((steps > 0) & (steps < last))
                def _():
                    def work(i):
                        i_own = pl.ds(pl.multiple_of(k * chunk + i, STEP), STEP)
                        i_at = pl.ds(pl.multiple_of(side * half + k * chunk + i, STEP), STEP)
                        go[side, i_own, :] = (
                            land[side, i_own, :].astype(f32) + part[i_at, :].astype(f32)
                        ).astype(bf16)

                    rows_loop(chunk, STEP, work)
                    env.copy(go.at[side, own, :], land.at[side, own, :], sem + k, there).start()

        def backward(tick, side):
            steps, there, back, sem, sem_back = layout(side)
            k = tick - start - HOP * (2 * last - steps)

            @pl.when(due(k) & (steps < last))
            def _():
                at, own = slices(side, k)
                env.arrived(out.at[at, :], sem_back + k)

                @pl.when(steps > 0)
                def _():
                    env.copy(out.at[at, :], out.at[at, :], sem_back + k, back).start()

        def tick_of(tick):
            for side in (0, 1):
                forward(tick, side)
            if spread:
                return
            for side in (0, 1):
                backward(tick, side)

        def drain():
            for side in (0, 1):
                steps, there, back, sem, sem_back = layout(side)

                def one(k, carry, side=side, steps=steps, sem=sem, sem_back=sem_back):
                    at, own = slices(side, k)
                    rows = out.at[at, :]
                    near = {"section": 1 - env.core}

                    @pl.when(steps < last)
                    def _():
                        env.copy(rows, rows, sem + k, near).wait_send()

                    if spread:
                        first = base_far + side * places * CHUNKS + k
                        sink = last if (side == 0) != flip else 0
                        away = lax.rem(env.place - sink + places, places)

                        @pl.when(steps == last)
                        def _():
                            for j in range(1, places):
                                sent = columns_at(at, lax.rem(env.place + j, places))
                                env.copy(sent, sent, first + j * CHUNKS, near).wait_send()

                        @pl.when(steps < last)
                        def _():
                            env.arrived(columns_at(at, env.place), first + away * CHUNKS)

                        return carry

                    @pl.when(steps > 0)
                    def _():
                        env.copy(rows, rows, sem_back + k, near).wait_send()

                    return carry

                lax.fori_loop(0, CHUNKS, one, 0)

        env.looped.append(tick_of)
        return [(-30, prepare), (2000, drain)]

    group.jobs.append(job)
    return n_out, n_keep, n_sums


def column_loop(count, tile, work):
    def one(j, carry):
        work(pl.ds(pl.multiple_of(j * tile, tile), tile))
        return carry

    lax.fori_loop(0, count // tile, one, 0)


def stream(group, produce, start, flip, chunks):
    last = lax.axis_size("tensor") - 1
    group.ticks = max(group.ticks, start + chunks + HOP * last)

    def job(env):
        count = env.rows

        def tick_of(tick):
            for side in (0, 1):
                right = (side == 0) != flip
                steps = env.place if right else last - env.place
                k = tick - start - HOP * steps

                @pl.when((k >= 0) & (k < chunks))
                def _():
                    half = count // 2
                    chunk = half // chunks
                    at = pl.ds(pl.multiple_of(side * half + k * chunk, STEP), chunk)
                    own = pl.ds(pl.multiple_of(k * chunk, STEP), chunk)
                    produce(env, side, k, at, own, steps == 0)

        env.looped.append(tick_of)
        return []

    group.jobs.append(job)


def feed_forward(source, kept, vectors, up, down, b_up, upper, active, part):
    def produce(env, side, k, at, own, first):
        rows, residual, vec, w_up, w_down = (
            env(source), env(kept), env(vectors), env(up), env(down),
        )
        bias, o_upper, o_active, o_part = env(b_up), env(upper), env(active), env(part)
        units, width = w_down.shape

        def widen(cols):
            value = dot(rows[at, :], w_up[:, cols], ((1,), (0,))) + bias[0:1, cols]
            o_upper[at, cols] = value
            bent = jnp.tanh(root * (value + cubic * (value * value * value)))
            o_active[at, cols] = (0.5 * value * (1.0 + bent)).astype(bf16)

        def narrow(cols):
            value = dot(o_active[at, :], w_down[:, cols], ((1,), (0,)))
            extra = jnp.where(first, residual[own, cols] + vec[5:6, cols], 0.0)
            o_part[at, cols] = (value + extra).astype(bf16)

        column_loop(units, min(TILE, units), widen)
        column_loop(width, TILE, narrow)

    return produce


def feed_back(source, up, down, upper, grad_upper, part):
    def produce(env, side, k, at, own, first):
        rows, w_up, w_down = env(source), env(up), env(down)
        i_upper, o_grad, o_part = env(upper), env(grad_upper), env(part)
        units, width = w_down.shape

        def widen(cols):
            value = i_upper[at, cols]
            square = value * value
            bent = jnp.tanh(root * (value + cubic * (value * square)))
            slope = 0.5 * (1.0 + bent) + 0.5 * value * (1.0 - bent * bent) * (
                root * (1.0 + 3.0 * cubic * square)
            )
            grad = dot(rows[at, :], w_down[cols, :], ((1,), (1,)))
            o_grad[at, cols] = (grad * slope).astype(bf16)

        def narrow(cols):
            value = dot(o_grad[at, :], w_up[cols, :], ((1,), (1,)))
            o_part[at, cols] = value.astype(bf16)

        column_loop(units, min(TILE, units), widen)
        column_loop(width, TILE, narrow)

    return produce


def gather_line(group, piece):
    count, width = piece.shape
    places = lax.axis_size("tensor")
    if width % 128:
        return None
    group.peers.add("line")
    n_in = group.operand(piece, pltpu.VMEM)
    n_out = group.result((count, width * places), piece.dtype, pltpu.VMEM)
    base = group.sems(places)

    def job(env):
        source, out = env(n_in), env(n_out)

        def columns(index):
            return out.at[:, pl.ds(pl.multiple_of(index * width, width), width)]

        def begin():
            for j in sorted(range(1, places), key=lambda j: -min(j, places - j)):
                env.start(source, columns(env.place), base + j, env.along(j))
            env.local(source, columns(env.place), base)

        def end():
            for j in range(1, places):
                env.arrived(columns(lax.rem(env.place - j + places, places)), base + j)

        return [(-10, begin), (900, end)]

    group.jobs.append(job)
    return n_out[1]


def gather_all(group, piece):
    rows, width = piece.shape
    quads, places = lax.axis_size("seq"), lax.axis_size("tensor")
    group.peers.update(("plane", "line"))
    n_in = group.operand(piece, pltpu.VMEM)
    n_out = group.result((2, quads, places, rows, width), piece.dtype, pltpu.VMEM)
    base = group.sems(quads + places + 1)

    def job(env):
        source, out = env(n_in), env(n_out)
        mine = out.at[env.core, env.quad, env.place]

        def begin():
            mine[...] = source[...]
            for j in range(1, places):
                env.start(mine, mine, base + j, env.along(j))

        def second():
            for j in range(1, places):
                there = lax.rem(env.place - j + places, places)
                env.arrived(out.at[env.core, env.quad, there], base + j)
            line = out.at[env.core, env.quad]
            for j in range(1, quads):
                env.start(line, line, base + places + j, env.peer(j, 0))

        def third():
            for j in range(1, quads):
                there = lax.rem(env.quad - j + quads, quads)
                env.arrived(out.at[env.core, there], base + places + j)
            env.start(out.at[env.core], out.at[env.core], base, env.peer(0, 1))

        def end():
            env.arrived(out.at[1 - env.core], base)

        return [(-20, begin), (90, second), (91, third), (903, end)]

    group.jobs.append(job)
    return n_out[1]


def piece_of(ref, axis, slot, first, rows, shard, width):
    if axis == 0:
        return ref.at[pl.ds(pl.multiple_of(slot * shard + first, 16), rows), :]
    if not isinstance(first, int):
        first = pl.multiple_of(first, 16)
    return ref.at[
        pl.ds(first, rows), pl.ds(pl.multiple_of(slot * width, width), width)
    ]


def gather_plane(group, layer, shard, axis, when, inject_at=-4):
    rows, width = shard.shape
    half = rows // 2
    quads = lax.axis_size("seq")
    group.peers.add("plane")
    full = (rows * quads, width) if axis == 0 else (rows, width * quads)
    n_in = group.operand(shard, pl.ANY)
    n_out = group.result(full, shard.dtype, pl.ANY)
    base = group.sems(3 * quads + 1)

    def job(env):
        source, out = env(n_in), env(n_out)
        holder = env.core == layer

        def part(slot, core):
            return piece_of(out, axis, slot, core * half, half, rows, width)

        def whole(slot):
            return piece_of(out, axis, slot, 0, rows, rows, width)

        other = jnp.logical_not(holder)
        slots = [lax.rem(env.quad - j + quads, quads) for j in range(quads)]
        mine = [part(slot, env.core) for slot in slots]
        theirs = [part(slot, env.other) for slot in slots]
        own_slot = whole(env.quad)
        halves = [source.at[pl.ds(core * half, half), :] for core in (0, 1)]
        placed = [part(env.quad, core) for core in (0, 1)]

        placed_here = part(env.quad, env.core)
        order = (2, 1, 3) if quads == 4 else range(1, quads)

        def begin():
            env.start(source, own_slot, base + quads, env.peer(0, 1), holder)
            env.local(source, own_slot, base, holder)
            for j in order:
                env.start(halves[layer], placed[layer], base + j, env.peer(j, 0), holder)

        def inject():
            pl.when(other)(lambda: env.arrived(own_slot, base + quads))
            for j in order:
                env.start(placed_here, placed_here, base + j, env.peer(j, 0), other)

        def pass_on():
            for j in range(1, quads):
                env.arrived(mine[j], base + j)
                env.start(mine[j], mine[j], base + 2 * quads + j, env.peer(0, 1))

        def end():
            for j in range(1, quads):
                env.arrived(theirs[j], base + 2 * quads + j)

        return [(-5, begin), (inject_at, inject), (when, pass_on), (901, end)]

    group.jobs.append(job)
    return n_out[1]


def reduce_plane(group, layer, grad, axis, times):
    quads = lax.axis_size("seq")
    rows = grad.shape[0] // quads if axis == 0 else grad.shape[0]
    width = grad.shape[1] if axis == 0 else grad.shape[1] // quads
    half = rows // 2
    step = 32
    group.peers.add("plane")
    n_in = group.operand(grad, pltpu.VMEM)
    n_out = group.result((rows, width), f32, pltpu.VMEM)
    n_land = group.room((quads, half, width), bf16)
    n_sum = group.room((quads, half, width), bf16)
    n_far = group.room((quads, half, width), bf16)
    n_fin = group.room((half, width), f32)
    base = group.sems(2 * quads + 1)

    def job(env):
        mine, out, land, total, far, fin = (
            env(n_in), env(n_out), env(n_land), env(n_sum), env(n_far), env(n_fin),
        )
        holder = env.core == layer
        other = jnp.logical_not(holder)
        order = [2, 1, 3, 0] if quads == 4 else list(range(1, quads)) + [0]
        slots = [lax.rem(env.quad + j, quads) for j in range(quads)]
        mine_of = [
            piece_of(mine, axis, slot, env.core * half, half, rows, width) for slot in slots
        ]
        their_of = [
            piece_of(mine, axis, slot, env.other * half, half, rows, width) for slot in slots
        ]
        lands = [land.at[slot] for slot in slots]
        totals = [total.at[slot] for slot in slots]
        fars = [far.at[j] for j in range(quads)]
        spot_mine = out.at[pl.ds(pl.multiple_of(env.core * half, 16), half), :]
        spot_other = out.at[pl.ds(pl.multiple_of(env.other * half, 16), half), :]

        def begin():
            for j in order:
                env.start(their_of[j], lands[j], base + j, env.peer(0, 1))

        def middle():
            for j in order:
                slot = slots[j]
                env.arrived(lands[j], base + j)
                own = mine_of[j]

                def work(i, slot=slot, own=own):
                    at = pl.ds(i, step)
                    total[slot, at, :] = (
                        own[at, :].astype(f32) + land[slot, at, :].astype(f32)
                    ).astype(bf16)

                rows_loop(half, step, work)
                if j:
                    env.start(totals[j], fars[j], base + quads + j, env.peer(j, 0))

        def close():
            for j in range(1, quads):
                env.arrived(far.at[j], base + quads + j)

            def work(i):
                at = pl.ds(i, step)
                value = total[env.quad, at, :].astype(f32)
                for j in range(1, quads):
                    value = value + far[j, at, :].astype(f32)
                fin[at, :] = value

            rows_loop(half, step, work)
            env.start(fin, spot_mine, base + 2 * quads, env.peer(0, 1), other)
            env.local(fin, spot_mine, base + quads, holder)

        def end():
            @pl.when(holder)
            def _():
                env.arrived(spot_other, base + 2 * quads)

        return [(times[2], begin), (times[0], middle), (times[1], close), (1500, end)]

    group.jobs.append(job)
    return n_out[1]


def sum_vectors(group, pair, shared, late):
    rows, width = pair.shape[1:]
    quads, places = lax.axis_size("seq"), lax.axis_size("tensor")
    group.peers.update(("plane", "line"))
    n_in = group.operand(pair, pltpu.VMEM)
    n_out = group.result((rows, width), f32, pltpu.VMEM)
    n_near = group.room((rows, width), f32)
    n_full = group.room((2, rows, width), f32)
    n_one = group.room((rows, width), f32)
    n_far = group.room((quads, rows, width), f32)
    n_two = group.room((rows, width), f32)
    n_end = group.room((places, rows, width), f32)
    base = group.sems(quads + places)

    def job(env):
        given, out, near, one, far, two, ends = (
            env(n_in), env(n_out), env(n_near), env(n_one), env(n_far), env(n_two), env(n_end),
        )
        mine = env(n_full)

        def go():
            mine[...] = given[...]
            for row in range(late[1]):
                extra = env(late[0])[row * 8 : row * 8 + 8, :]
                mine[0, row : row + 1, :] = jnp.sum(extra, axis=0, keepdims=True)
            env.start(mine.at[1 - env.core], near, base, env.peer(0, 1))
            env.arrived(near, base)
            one[...] = mine[env.core] + near[...]
            for j in range(1, quads):
                env.start(one, far.at[j], base + j, env.peer(j, 0))
            value = one[...]
            for j in range(1, quads):
                env.arrived(far.at[j], base + j)
                value = value + far[j]
            two[...] = value
            for j in range(1, places):
                env.start(two, ends.at[j], base + quads + j, env.along(j))
            for j in range(1, places):
                env.arrived(ends.at[j], base + quads + j)
                value = value + ends[j]
            row = lax.broadcasted_iota(jnp.int32, value.shape, 0)
            out[...] = jnp.where(row < shared, value, two[...])

        return [(890, go)]

    group.jobs.append(job)
    return n_out[1]


def allowed_mask(segment):
    length = segment.shape[1]
    place = lax.broadcasted_iota(jnp.int32, (length, length), 0)
    other = lax.broadcasted_iota(jnp.int32, (length, length), 1)
    same = segment[:, :, None] == segment[:, None, :]
    return (same & (other <= place)[None])[:, None]


def dot(left, right, dims):
    return lax.dot_general(left, right, (dims, ((), ())), preferred_element_type=f32)


def attend(whole, mask, gain, bias, w_qkv, b_qv, w_out, heads):
    count = whole.shape[0]
    size = w_qkv.shape[1] // heads // 3
    shape4 = (mask.shape[0], mask.shape[2], heads, size)
    factor = 1.0 / math.sqrt(size)
    normed = (statistics(whole.astype(f32))[0] * gain + bias).astype(bf16)
    mixed = dot(normed, w_qkv, ((1,), (0,))).reshape(count, heads, 3 * size)
    query = (mixed[..., :size] + b_qv[:, :size]).astype(bf16).reshape(shape4)
    keys = mixed[..., size : 2 * size].astype(bf16).reshape(shape4)
    values = (mixed[..., 2 * size :] + b_qv[:, size:]).astype(bf16).reshape(shape4)
    scores = jnp.einsum("sqhe,skhe->shqk", query, keys, preferred_element_type=f32) * factor
    masked = jnp.where(mask, scores, floor_value)
    raised = jnp.exp(masked - jnp.max(masked, axis=-1, keepdims=True))
    chance = raised / jnp.sum(raised, axis=-1, keepdims=True)
    low = chance.astype(bf16)
    context = jnp.einsum("shqk,skhe->sqhe", low, values, preferred_element_type=f32)
    context = context.reshape(count, heads * size).astype(bf16)
    partial = dot(context, w_out, ((1,), (0,))).astype(bf16)
    return (partial, (normed, query, keys, values, chance, low, context))


def attend_back(whole_ga, kept, w_qkv, w_out):
    normed, query, keys, values, chance, low, context = kept
    count = whole_ga.shape[0]
    heads, size = query.shape[2:]
    factor = 1.0 / math.sqrt(size)
    grad_context = dot(whole_ga, w_out, ((1,), (1,))).astype(bf16).reshape(query.shape)
    grad_chance = jnp.einsum("sqhe,skhe->shqk", grad_context, values, preferred_element_type=f32)
    delta = jnp.sum(grad_chance * chance, axis=-1, keepdims=True)
    grad_scores = (chance * (grad_chance - delta)).astype(bf16)
    grad_query = (
        jnp.einsum("shqk,skhe->sqhe", grad_scores, keys, preferred_element_type=f32) * factor
    ).astype(bf16)
    grad_keys = (
        jnp.einsum("shqk,sqhe->skhe", grad_scores, query, preferred_element_type=f32) * factor
    ).astype(bf16)
    grad_values = jnp.einsum(
        "shqk,sqhe->skhe", low, grad_context, preferred_element_type=f32
    ).astype(bf16)
    grad_mixed = jnp.concatenate([grad_query, grad_keys, grad_values], axis=-1).reshape(
        count, heads * 3 * size
    )
    partial = dot(grad_mixed, w_qkv, ((1,), (1,))).astype(bf16)
    grad_out_w = dot(context, whole_ga, ((0,), (0,))).astype(bf16)
    grad_qkv = dot(normed, grad_mixed, ((0,), (0,))).astype(bf16)
    grad_qv = jnp.concatenate(
        [
            jnp.sum(grad_query.astype(f32), axis=(0, 1)),
            jnp.sum(grad_values.astype(f32), axis=(0, 1)),
        ],
        axis=-1,
    )
    return (partial, grad_out_w, grad_qkv, grad_qv)


def swap(item):
    return lax.ppermute(item, "section", [(0, 1), (1, 0)])


def body(
    tokens, segments, cotangent, norm1_gain, norm1_bias, qkv_weight, qv_bias, out_weight, out_bias,
    norm2_gain, norm2_bias, up_weight, up_bias, down_weight, down_bias,
):
    section = lax.axis_index("section")
    place = lax.axis_index("tensor")
    quad = lax.axis_index("seq")
    tensors = lax.axis_size("tensor")
    quads = lax.axis_size("seq")
    first = section == 0
    rows_all, width = tokens.shape
    full = width * tensors
    heads, wide = qkv_weight.shape[2:]
    size = wide // 3
    part = norm1_gain.shape[1]
    part_up = up_bias.shape[1]
    part_qv = qv_bias.shape[2]
    hidden_units = up_weight.shape[2]

    def mine(item):
        return lax.dynamic_slice_in_dim(item, section * (item.shape[0] // 2), item.shape[0] // 2, 0)

    def columns_of(whole):
        return lax.dynamic_slice_in_dim(whole, place * width, width, 1)

    packed = jnp.concatenate(
        [
            norm1_gain[0], norm1_bias[0], out_bias[0], norm2_gain[0], norm2_bias[0], down_bias[0],
            up_bias[0], qv_bias[0].reshape(-1),
        ]
    )
    length = packed.shape[0]
    packed = jnp.pad(packed.astype(f32), (0, -length % 1024)).reshape(-1, 128)

    def vectors_of(layer):
        own = small[layer]
        vectors = [own[:, :, i * part : (i + 1) * part].reshape(1, full) for i in range(6)]
        local = lax.dynamic_slice_in_dim(own, place, 1, 0)[0]
        b_up = local[:, 6 * part : 6 * part + part_up].reshape(-1)
        b_qv = local[:, 6 * part + part_up :].reshape(quads, heads, part_qv)
        b_qv = jnp.transpose(b_qv, (1, 0, 2)).reshape(heads, 2 * size)
        return (vectors, b_up, b_qv)

    def block(*rows):
        return jnp.concatenate(
            list(rows) + [jnp.zeros((8 - len(rows), full), f32)], axis=0
        )

    shards = (
        (qkv_weight[0].reshape(-1, heads * wide), 0),
        (out_weight[0].reshape(heads * size, -1), 1),
        (up_weight[0], 0),
        (down_weight[0], 1),
    )
    mask = allowed_mask(mine(segments))

    def whole_of(index, item):
        if index is None:
            return lax.all_gather(mine(item), "tensor", axis=1, tiled=True)
        return got[index]

    start = Group(0)
    at_v = gather_all(start, packed)
    at_x = gather_line(start, mine(tokens))
    at_w = [gather_plane(start, 0, item, axis, 100 + i) for i, (item, axis) in enumerate(shards)]
    got = start.run()
    small = jnp.transpose(got[at_v].reshape(2, quads, tensors, -1)[..., :length], (0, 2, 1, 3))
    whole0 = whole_of(at_x, tokens)
    cot = lax.all_gather(mine(cotangent), "tensor", axis=1, tiled=True)
    weights0 = [got[i] for i in at_w]
    vec0, b_up0, b_qv0 = vectors_of(0)
    vec1, b_up1, b_qv1 = vectors_of(1)

    def branch(call, source, weights, b_up, kept, vectors, flip, chain=True):
        up, down = name_of(call, weights[2]), name_of(call, weights[3])
        shape = (whole0.shape[0], weights[2].shape[1])
        upper = call.result(shape, f32, pltpu.VMEM)
        active = call.result(shape, bf16, pltpu.VMEM)
        if chain:
            out_part = call.room(whole0.shape, bf16)
        else:
            out_part = call.result(whole0.shape, bf16, pltpu.VMEM)
        produce = feed_forward(
            source, kept, vectors, up, down, name_of(call, b_up.reshape(1, -1)), upper, active,
            out_part,
        )
        if not chain:
            call.rows = whole0.shape[0]
            stream(call, produce, hop, flip, CHUNKS)
            return out_part, upper, active, up, down
        made = chain_sum(call, "f2", out_part, None, flip=flip, start=hop, produce=produce)
        return made[0], upper, active, up, down

    def branch_back(call, source, up, down, upper, vectors, kept, flip, start):
        shape = (whole0.shape[0], units)
        grad_upper = call.result(shape, bf16, pltpu.VMEM)
        back_part = call.room(whole0.shape, bf16)
        produce = feed_back(source, up, down, upper, grad_upper, back_part)
        made = chain_sum(
            call, "b1", back_part, vectors, flip=flip, start=start, produce=produce, wide=source,
            kept=kept,
        )
        return made + (grad_upper,)

    def branch_grads(normed2, active, upstream, grad_upper):
        return (
            dot(normed2, grad_upper, ((0,), (0,))).astype(bf16),
            dot(active, upstream, ((0,), (0,))).astype(bf16),
            jnp.sum(grad_upper.astype(f32), axis=0),
        )

    units = hidden_units
    hop = HOP * (tensors - 1)

    partial, kept_a0 = attend(whole0, mask, vec0[0], vec0[1], weights0[0], b_qv0, weights0[1], heads)
    call = Group(1)
    at_v = call.operand(block(vec0[2], vec0[3], vec0[4], vec0[3], vec0[0], vec0[5]), pltpu.VMEM)
    a = chain_sum(call, "f1", partial, at_v, flip=True, wide=whole0)
    b = branch(call, a[0], weights0, b_up0, a[1], at_v, False)
    at_w2 = [
        gather_plane(call, 1, *shards[i], when=when, inject_at=2 * HOP)
        for i, when in zip(range(4), (hop + 1, hop + 2, 2 * hop + 1, 2 * hop + 2))
    ]
    got = call.run()
    normed2_0, hidden0, whole1, upper0, active0 = (got[i[1]] for i in (a[0], a[1]) + b[:3])
    weights1 = [got[i] for i in at_w2]

    partial, kept_a1 = attend(
        whole1, mask, vec1[0], vec1[1], weights1[0], b_qv1, weights1[1], heads
    )
    call = Group(2)
    at_v = call.operand(block(vec1[2], vec1[3], vec1[4], vec1[3], vec1[0], vec1[5]), pltpu.VMEM)
    a = chain_sum(call, "f1", partial, at_v, wide=whole1)
    b = branch(call, a[0], weights1, b_up1, a[1], at_v, True, chain=False)
    at_cot = call.operand(cot, pltpu.VMEM)
    c = branch_back(
        call, at_cot, b[3], b[4], b[1], call.operand(block(vec1[3]), pltpu.VMEM), a[1], False,
        2 * hop,
    )
    got = call.run()
    normed2_1, last_part, active1 = (got[i[1]] for i in (a[0], b[0], b[2]))
    columns2 = lax.psum_scatter(last_part, "tensor", scatter_dimension=1, tiled=True)
    ga, dhidden, sums_b1, grad_upper1 = (got[i[1]] for i in c)
    g_up1, g_down1, s_up1 = branch_grads(normed2_1, active1, cot, grad_upper1)

    partial, g_out1, g_qkv1, s_qv1 = attend_back(ga, kept_a1, weights1[0], weights1[1])
    call = Group(3)
    a = chain_sum(call, "b2", partial, block(vec1[0]), wide=whole1, kept=dhidden)
    c = branch_back(
        call, a[0], name_of(call, weights0[2]), name_of(call, weights0[3]), name_of(call, upper0),
        call.operand(block(vec0[3]), pltpu.VMEM), name_of(call, hidden0), True, hop,
    )
    at_g = [
        reduce_plane(call, 1, item, axis, (first_at, 2 * hop + 3, begin_at))
        for item, axis, first_at, begin_at in (
            (g_up1, 0, 1, -8), (g_down1, 1, 2, 1), (g_qkv1, 0, 3, 2), (g_out1, 1, 3, 2)
        )
    ]
    got = call.run()
    grad1, sums_b2 = got[a[0][1]], got[a[2][1]]
    ga, dhidden, sums_a1, grad_upper0 = (got[i[1]] for i in c)
    r_up1, r_down1, r_qkv1, r_out1 = (got[i] for i in at_g)
    g_up0, g_down0, s_up0 = branch_grads(normed2_0, active0, grad1, grad_upper0)

    partial, g_out0, g_qkv0, s_qv0 = attend_back(ga, kept_a0, weights0[0], weights0[1])
    def rows_of(sums_one, sums_two, up, qv):
        one = jnp.sum(sums_one.reshape(4, 8, full), axis=1)
        two = jnp.sum(sums_two.reshape(2, 8, full), axis=1)
        flat = [
            jnp.pad(item.reshape(1, -1), ((0, 0), (0, full - item.size))) for item in (up, qv)
        ]
        return jnp.concatenate([two, one[2:3], one[0:2], one[3:4]] + flat, axis=0)

    small_sums = jnp.stack(
        [
            rows_of(sums_a1, jnp.zeros((16, full), f32), s_up0, s_qv0),
            rows_of(sums_b1, sums_b2, s_up1, s_qv1),
        ]
    )
    call = Group(4)
    a = chain_sum(call, "b2", partial, block(vec0[0]), flip=True, wide=whole0, kept=dhidden, spread=True)
    at_g = [
        reduce_plane(call, 0, item, axis, (first_at, 1000, begin_at))
        for item, axis, first_at, begin_at in (
            (g_up0, 0, 1, -8), (g_down0, 1, 3, 2), (g_qkv0, 0, 5, 4), (g_out0, 1, 5, 4)
        )
    ]
    at_v = sum_vectors(call, small_sums, 6, (a[2], 2))
    got = call.run()
    grad0, vectors = got[a[0][1]], got[at_v]
    r_up0, r_down0, r_qkv0, r_out0 = (got[i] for i in at_g)

    spot = (place * quads + quad) * part
    small_grads = [lax.dynamic_slice(vectors, (i, spot), (1, part))[0] for i in range(6)]
    g_up = lax.dynamic_slice(vectors, (6, quad * part_up), (1, part_up))[0]
    g_qv = vectors[7, : heads * 2 * size].reshape(heads, quads, part_qv)
    g_qv = lax.dynamic_slice_in_dim(g_qv, quad, 1, 1)[:, 0]

    def settle(of0, of1):
        own = jnp.where(first, of0, of1)
        other = swap(jnp.where(first, of1, of0))
        return jnp.where(
            first, jnp.concatenate([own, other]), jnp.concatenate([other, own])
        )

    outputs = settle(columns_of(whole1), columns2)
    input_grads = settle(columns_of(grad0), columns_of(grad1))
    totals = [
        jnp.where(first, one, two)
        for one, two in ((r_qkv0, r_qkv1), (r_out0, r_out1), (r_up0, r_up1), (r_down0, r_down1))
    ]
    result = (
        outputs,
        input_grads,
        small_grads[0],
        small_grads[1],
        totals[0].reshape(-1, heads, wide),
        g_qv,
        totals[1].reshape(heads, size, -1),
        small_grads[2],
        small_grads[3],
        small_grads[4],
        totals[2],
        g_up,
        totals[3],
        small_grads[5],
    )
    return tuple(item[None] for item in result)


def solution(mesh):
    vector = P("section", ("tensor", "seq"))
    return jax.shard_map(
        body,
        mesh=mesh,
        in_specs=(
            P("seq", "tensor"),
            P("seq", None),
            P("seq", "tensor"),
            vector,
            vector,
            P("section", "seq", "tensor", None),
            P("section", "tensor", "seq"),
            P("section", "tensor", None, "seq"),
            vector,
            vector,
            vector,
            P("section", "seq", "tensor"),
            vector,
            P("section", "tensor", "seq"),
            vector,
        ),
        out_specs=(
            P("section", "seq", "tensor"),
            P("section", "seq", "tensor"),
            vector,
            vector,
            P("section", "seq", "tensor", None),
            P("section", "tensor", "seq"),
            P("section", "tensor", None, "seq"),
            vector,
            vector,
            vector,
            P("section", "seq", "tensor"),
            vector,
            P("section", "tensor", "seq"),
            vector,
        ),
        check_vma=False,
    )
```
